256 devices in a mesh: row: 32 (over x, y, core), col: 8 (over z).
Axes of the slice: x: 4, y: 4, z: 8, core: 2. Of those that a mesh axis runs over, the one named last changes fastest.
Arguments:
- rhs: float32 [4, 2048, 1024], P(None, 'row', 'col'), may hold values from -6 to 6
- l_panel: bfloat16 [4, 2048, 32768], P(None, 'row', 'col'), may hold values from -0.03125 to 0.03125
- x_solved: bfloat16 [32768, 1024], P('col'), may hold values from -6 to 6
- diag_inv: bfloat16 [4, 2048, 2048], P(None, 'row'), may hold values from -1 to 1.5, as said below
- l_inner: bfloat16 [6, 2048, 2048], P(None, 'row'), may hold values from -0.0625 to 0.0625
Outputs:
- x_window: float32 [4, 2048, 1024], P(None, 'row', 'col')
The draws below stay inside these ranges and needn't reach their ends.
Inputs may be any that keep to these rules, and one draw needn't show every extreme that they name: `diag_inv`: each block is lower triangular with diagonal entries between one half and three halves.
All inputs are finite; a program needn't handle non-finite values.
Results may differ from the reference program's by a relative error of at most 0.0045.
Values may be sent and summed in bfloat16 or wider, within the bound.
A program may use at most 64 MiB of HBM per device.

```python
import math
import jax
import jax.numpy as jnp
from jax import lax

NRHS = 1024
BLK = 2048
STEPS = 4
SOLVED = 32768
PAIRS = 6


def draw_diag_inv(key, part):
    key_diag, key_off = jax.random.split(jax.random.fold_in(key, 11))
    shape = (STEPS, BLK, BLK)
    row_ids = lax.broadcasted_iota(jnp.int32, shape, 1)
    col_ids = lax.broadcasted_iota(jnp.int32, shape, 2)
    diagonal = jax.random.uniform(key_diag, shape, jnp.float32, 0.6, 1.4)
    lower = jnp.clip(jax.random.normal(key_off, shape, jnp.float32), -4.0, 4.0) * (0.6 / math.sqrt(BLK))
    values = jnp.where(row_ids == col_ids, diagonal, jnp.where(col_ids < row_ids, lower, 0.0))
    return values.astype(jnp.bfloat16)


def raised(result, key, source, target, blocks, factor):
    owner, partner = [(jnp.arange(result.shape[position]) // (result.shape[position] // blocks)).reshape([-1 if axis == position else 1 for axis in range(result.ndim)]) for position in (source, target)]
    chosen = jax.random.permutation(key, blocks)[partner]
    strong = (owner == chosen) | (owner == (partner + blocks // 2) % blocks)
    return jnp.where(strong, factor * result, result)


def block_scale(own_key, shape, pieces, smallest, top_value):
    gain, own = 1.0, jax.random.fold_in(own_key, 6)
    for dim, blocks in pieces:
        heights = jnp.exp(jax.random.uniform(jax.random.fold_in(own, dim), (blocks,), jnp.float32, smallest / len(pieces), top_value / len(pieces)))
        gain = gain * jnp.repeat(heights, shape[dim] // blocks).reshape([-1 if axis == dim else 1 for axis in range(len(shape))])
    return gain


def noise(key, shape, scale, bound, pieces=(), dtype=jnp.bfloat16):
    level = block_scale(key, shape, pieces, -0.22, 0.18) if pieces else 1.0
    result = jax.random.normal(key, shape, jnp.float32) * scale * level
    return jnp.minimum(jnp.maximum(result, -bound), bound).astype(dtype)


def noise_with(rng, dims, deviation, bound, pieces, heavy, dtype=jnp.bfloat16):
    entries = deviation * jax.random.normal(rng, dims, jnp.float32)
    if pieces:
        entries = entries * block_scale(rng, dims, pieces, -0.22, 0.18)
    return jnp.clip(raised(entries, jax.random.fold_in(rng, 3), *heavy), -bound, bound).astype(dtype)


def setup_inputs(seed: int = 0) -> dict:
    streams_of = jax.random.split(jax.random.key(seed), 6)
    return {
        "rhs": noise(streams_of[0], (STEPS, BLK, NRHS), 1.0, 6.0, ((1, 32), (2, 8)), jnp.float32),
        "l_panel": noise(streams_of[1], (STEPS, BLK, SOLVED), SOLVED ** -0.5, 0.03125, ((1, 32), (2, 8))),
        "x_solved": noise_with(streams_of[2], (SOLVED, NRHS), 1.0, 6.0, ((0, 8),), (0, 1, 8, 2.0)),
        "diag_inv": draw_diag_inv(jax.random.fold_in(streams_of[5], 71), 0),
        "l_inner": noise(streams_of[4], (PAIRS, BLK, BLK), (4 * BLK) ** -0.5, 0.0625, ((1, 32),)),
    }


def reference(rhs, l_panel, x_solved, diag_inv, l_inner):
    solved_low = []
    results = []
    for target in range(STEPS):
        products = jnp.dot(l_panel[target], x_solved, preferred_element_type=jnp.float32)
        resid = rhs[target] - products
        for earlier in range(target):
            resid = resid - jnp.dot(l_inner[target * (target - 1) // 2 + earlier], solved_low[earlier], preferred_element_type=jnp.float32)
        current = jnp.dot(diag_inv[target], resid.astype(jnp.bfloat16), preferred_element_type=jnp.float32)
        results.append(current)
        solved_low.append(current.astype(jnp.bfloat16))
    return jnp.stack(results, axis=0)
```

```python
import jax
import jax.numpy as jnp
from jax import lax
from jax.experimental import pallas as pl
from jax.experimental.pallas import tpu as pltpu
from jax.sharding import PartitionSpec as P

MESH = pl.DeviceIdType.MESH
BF = jnp.bfloat16
F32 = jnp.float32


def dot(a, b):
    return jnp.dot(a, b, preferred_element_type=F32)


def inner_index(target, earlier):
    return target * (target - 1) // 2 + earlier


PLANE = sorted(
    [
        (min(dx, 4 - dx) + min(dy, 4 - dy), dx, dy, dc)
        for dx in range(4)
        for dy in range(4)
        for dc in range(2)
        if (dx, dy, dc) != (0, 0, 0)
    ],
    reverse=True,
)


def kernel(rhs, panel, solved, dinv, inner, out, lp, xs, dv, lv, rv, own, part, rs, g, pend,
           in_sem, rs_send, rs_recv, g_send, g_recv):
    r = lax.axis_index("row")
    c = lax.axis_index("col")
    core = r % 2
    y = (r // 2) % 4
    x = r // 8

    loads = [pltpu.make_async_copy(panel, lp, in_sem.at[0])]
    for i in range(4):
        for half, off in enumerate((4 + i, 3 - i)):
            dest = (c + off) % 8
            loads.append(
                pltpu.make_async_copy(
                    solved.at[:, pl.ds(pl.multiple_of(dest * 128, 128), 128)],
                    xs.at[i, :, pl.ds(128 * half, 128)],
                    in_sem.at[1 + 2 * i + half],
                )
            )
    loads.append(pltpu.make_async_copy(rhs, rv, in_sem.at[9]))
    loads.append(pltpu.make_async_copy(dinv, dv, in_sem.at[10]))
    loads.append(pltpu.make_async_copy(inner, lv, in_sem.at[11]))
    for cp in loads:
        cp.start()

    targets = []
    for _, dx, dy, dc in PLANE:
        targets.append((((x + dx) % 4) * 4 + (y + dy) % 4) * 2 + (core + dc) % 2)

    barrier = pltpu.get_barrier_semaphore()
    for off in range(1, 8):
        pl.semaphore_signal(barrier, inc=1, device_id=(r, (c + off) % 8), device_id_type=MESH)
    for t in targets:
        pl.semaphore_signal(barrier, inc=1, device_id=(t, c), device_id_type=MESH)

    def rs_copy(off, m):
        return pltpu.make_async_remote_copy(
            src_ref=part.at[off, m],
            dst_ref=rs.at[m, off - 1],
            send_sem=rs_send,
            recv_sem=rs_recv.at[m],
            device_id=(r, (c + off) % 8),
            device_id_type=MESH,
        )

    loads[0].wait()
    for i in range(4):
        loads[1 + 2 * i].wait()
        loads[2 + 2 * i].wait()
        acc = dot(lp[...].reshape(256, 4096), xs[i]).reshape(4, 64, 256)
        part[4 + i] = acc[:, :, :128].astype(BF)
        if i < 3:
            part[3 - i] = acc[:, :, 128:].astype(BF)
        else:
            own[...] = acc[:, :, 128:]
        if i == 0:
            pl.semaphore_wait(barrier, 38)
        rs_copy(4 + i, 0).start()
        if i < 3:
            rs_copy(3 - i, 0).start()
    for m in range(1, 4):
        for off in (4, 5, 3, 6, 2, 7, 1):
            rs_copy(off, m).start()

    mine = pl.ds(pl.multiple_of(r * 64, 64), 64)

    def reduce(m):
        pltpu.make_async_copy(rs.at[m], rs.at[m], rs_recv.at[m]).wait()
        total = own[m]
        for s in range(7):
            total = total + rs[m, s].astype(F32)
        return rv[m] - total

    def spread(n, value):
        g[n, mine, :] = value.astype(BF)
        for t in targets:
            pltpu.make_async_remote_copy(
                src_ref=g.at[n, mine],
                dst_ref=g.at[n, mine],
                send_sem=g_send.at[n],
                recv_sem=g_recv.at[n],
                device_id=(t, c),
                device_id_type=MESH,
            ).start()

    def arrived(n):
        pltpu.make_async_copy(
            g.at[n, pl.ds(0, 1984)], g.at[n, pl.ds(0, 1984)], g_recv.at[n]
        ).wait()

    loads[9].wait()
    resid = reduce(0)
    later = []
    for m in range(4):
        spread(2 * m if m < 3 else 6, resid)
        if m == 0:
            loads[10].wait()
            loads[11].wait()
            for k in range(1, 4):
                pend[k] = reduce(k)
        for target, n in later:
            pend[target] = pend[target] - dot(lv[inner_index(target, m - 1)], g[n])
        later = []
        arrived(2 * m)
        cur = dot(dv[m], g[2 * m])
        if m < 3:
            spread(2 * m + 1, cur)
        out[m] = cur
        if m < 3:
            arrived(2 * m + 1)
            resid = pend[m + 1] - dot(lv[inner_index(m + 1, m)], g[2 * m + 1])
            later = [(k, 2 * m + 1) for k in range(m + 2, 4)]

    pltpu.make_async_copy(part.at[pl.ds(1, 7)], part.at[pl.ds(1, 7)], rs_send).wait()
    for n in range(7):
        pltpu.make_async_copy(
            g.at[n, pl.ds(0, 1984)], g.at[n, pl.ds(0, 1984)], g_send.at[n]
        ).wait()


def local(rhs, l_panel, x_solved, diag_inv, l_inner):
    any_spec = pl.BlockSpec(memory_space=pl.ANY)
    return pl.pallas_call(
        kernel,
        out_shape=jax.ShapeDtypeStruct((4, 64, 128), F32),
        in_specs=[any_spec] * 5,
        out_specs=pl.BlockSpec(memory_space=pltpu.VMEM),
        scratch_shapes=[
            pltpu.VMEM((4, 64, 4096), BF),
            pltpu.VMEM((4, 4096, 256), BF),
            pltpu.VMEM((4, 64, 2048), BF),
            pltpu.VMEM((6, 64, 2048), BF),
            pltpu.VMEM((4, 64, 128), F32),
            pltpu.VMEM((4, 64, 128), F32),
            pltpu.VMEM((8, 4, 64, 128), BF),
            pltpu.VMEM((4, 7, 64, 128), BF),
            pltpu.VMEM((7, 2048, 128), BF),
            pltpu.VMEM((4, 64, 128), F32),
            pltpu.SemaphoreType.DMA((12,)),
            pltpu.SemaphoreType.DMA,
            pltpu.SemaphoreType.DMA((4,)),
            pltpu.SemaphoreType.DMA((7,)),
            pltpu.SemaphoreType.DMA((7,)),
        ],
        compiler_params=pltpu.CompilerParams(
            collective_id=0, has_side_effects=True, vmem_limit_bytes=60 * 1024 * 1024
        ),
    )(rhs, l_panel, x_solved, diag_inv, l_inner)


def solution(mesh):
    in_specs = (
        P(None, "row", "col"),
        P(None, "row", "col"),
        P("col", None),
        P(None, "row", None),
        P(None, "row", None),
    )
    return jax.shard_map(
        local, mesh=mesh, in_specs=in_specs, out_specs=P(None, "row", "col"), check_vma=False
    )
```

```python
import jax
import jax.numpy as jnp
from jax import lax
from jax.experimental import pallas as pl
from jax.experimental.pallas import tpu as pltpu
from jax.sharding import PartitionSpec as P

MESH = pl.DeviceIdType.MESH
BF = jnp.bfloat16
F32 = jnp.float32


def dot(a, b):
    return jnp.dot(a, b, preferred_element_type=F32)


NEXT = (0, 2, 5)
OTHER = {(2, 0): (0, 1), (3, 0): (1, 3), (3, 1): (2, 4)}

CHIPS = sorted(
    [(dx, dy) for dx in range(4) for dy in range(4) if (dx, dy) != (0, 0)],
    key=lambda t: -(min(t[0], 4 - t[0]) + min(t[1], 4 - t[1])),
)


def local_copy(src, dst, sem):
    return pltpu.make_async_copy(src, dst, sem)


def settle(ref, sem):
    pltpu.make_async_copy(ref, ref, sem).wait()


def kernel(
    rhs, panel, solved, dinv, inner, out,
    lp, xs, dv, dq, lm, mk, lx, dx_w, rv, own, part, rs, st, ga, xout, xin, pend, pre,
    in_sem, rs_send, rs_recv, g_send, g_recv, d_send, d_recv, m_send, m_recv, w_send, w_recv,
    x_send, x_recv,
):
    r = lax.axis_index("row")
    c = lax.axis_index("col")
    k = r % 2
    p = r // 2
    y = p % 4
    x = p // 4
    home = x // 2
    mine = pl.multiple_of(1024 * k, 1024)
    other = pl.multiple_of(1024 * (1 - k), 1024)
    sib = (2 * p + 1 - k, c)
    chips = [((x + dx) % 4) * 4 + (y + dy) % 4 for dx, dy in CHIPS]

    def send(src, dst, ssem, rsem, dev):
        pltpu.make_async_remote_copy(
            src_ref=src, dst_ref=dst, send_sem=ssem, recv_sem=rsem,
            device_id=dev, device_id_type=MESH,
        ).start()

    d_load = [local_copy(dinv.at[j], dv.at[j], in_sem.at[10 + j]) for j in range(3)]
    p_load = local_copy(panel, lp, in_sem.at[0])
    x_load = []
    for i in range(4):
        for half, off in enumerate((4 + i, 3 - i)):
            dest = (c + off) % 8
            x_load.append(
                local_copy(
                    solved.at[:, pl.ds(pl.multiple_of(dest * 128, 128), 128)],
                    xs.at[i, :, pl.ds(128 * half, 128)],
                    in_sem.at[1 + 2 * i + half],
                )
            )
    d_load[0].start()
    p_load.start()
    for cp in x_load:
        cp.start()
    r_load = local_copy(rhs, rv, in_sem.at[9])
    r_load.start()
    d_load[1].start()
    d_load[2].start()
    w_load = []
    for i in range(3):
        w_load.append(local_copy(inner.at[NEXT[i]], lm.at[i, 1], in_sem.at[13 + i]))
    for i, n in OTHER.values():
        w_load.append(local_copy(inner.at[n, :, pl.ds(mine, 1024)], lx.at[i, 1], in_sem.at[16 + i]))
    for m in range(4):
        w_load.append(
            local_copy(dinv.at[m, :, pl.ds(mine, 1024)], dx_w.at[m, 1], in_sem.at[19 + m])
        )
    for cp in w_load:
        cp.start()

    barrier = pltpu.get_barrier_semaphore()
    for off in range(1, 8):
        pl.semaphore_signal(barrier, inc=1, device_id=(r, (c + off) % 8), device_id_type=MESH)
    pl.semaphore_signal(barrier, inc=1, device_id=sib, device_id_type=MESH)
    for q in chips:
        for core in range(2):
            pl.semaphore_signal(barrier, inc=1, device_id=(2 * q + core, c), device_id_type=MESH)

    slice_of = lambda core: jnp.where(core == 0, c, 15 - c)
    my_slice = slice_of(k)
    my_local = pl.multiple_of((my_slice - 8 * k) * 128, 128)

    @pl.loop(0, my_slice)
    def _(i):
        rows = pl.ds(pl.multiple_of(i * 128, 128), 128)
        for j in range(3):
            dq[j, rows, :] = jnp.zeros((128, 128), BF)

    def send_inverse(j):
        rows = pl.ds(pl.multiple_of(r * 64, 64), 64)
        for d in range(2):
            core = (k + d) % 2
            s = slice_of(core)
            src = dv.at[j, :, pl.ds(pl.multiple_of(s * 128, 128), 128)]
            dst = dq.at[j, rows]

            @pl.when(p >= s)
            def _():
                for q in chips:
                    send(src, dst, d_send.at[j], d_recv.at[j], (2 * q + core, c))
                if d == 0:
                    local_copy(src, dst, d_recv.at[j]).start()
                else:
                    send(src, dst, d_send.at[j], d_recv.at[j], sib)

    def sent_inverse(j):
        near, far = p >= slice_of(k), p >= slice_of(1 - k)
        for rows, cond in (
            (1984, near & far),
            (960, near & jnp.logical_not(far)),
            (1024, far & jnp.logical_not(near)),
        ):

            @pl.when(cond)
            def _():
                settle(dq.at[j, pl.ds(0, rows)], d_send.at[j])

    def got_inverse(j):
        for s in range(16):

            @pl.when(my_slice == s)
            def _():
                settle(dq.at[j, pl.ds(128 * s, 2048 - 128 * s)], d_recv.at[j])

    def send_weights():
        for i in range(3):
            send(inner.at[NEXT[i]], lm.at[i, 0], w_send.at[0], w_recv.at[i], sib)
        for m in range(4):
            send(dinv.at[m, :, pl.ds(other, 1024)], dx_w.at[m, 0], w_send.at[1], w_recv.at[4], sib)
        for i, n in OTHER.values():
            send(inner.at[n, :, pl.ds(other, 1024)], lx.at[i, 0], w_send.at[2], w_recv.at[3], sib)

    def make_next(i):
        got_inverse(i)
        w_load[i].wait()
        settle(lm.at[i, 0], w_recv.at[i])
        block = dot(lm[i].reshape(128, 2048), dq[i])
        cols = pl.ds(my_local, 128)
        mk[i, :, cols] = block.astype(BF)
        for off in (4, 5, 3, 6, 2, 7, 1):
            send(mk.at[i, :, cols], mk.at[i, :, cols], m_send.at[i], m_recv.at[i], (r, (c + off) % 8))

    def rs_send_one(off, m):
        send(part.at[off, m], rs.at[m, off - 1], rs_send, rs_recv.at[m], (r, (c + off) % 8))

    def rs_send_all(m):
        for off in (4, 5, 3, 6, 2, 7, 1):
            rs_send_one(off, m)

    p_load.wait()
    for i in range(4):
        x_load[2 * i].wait()
        x_load[2 * i + 1].wait()
        acc = dot(lp[...].reshape(256, 4096), xs[i]).reshape(4, 64, 256)
        part[4 + i] = acc[:, :, :128].astype(BF)
        if i < 3:
            part[3 - i] = acc[:, :, 128:].astype(BF)
        else:
            own[...] = acc[:, :, 128:]
        if i == 0:
            pl.semaphore_wait(barrier, 38)
            d_load[0].wait()
            send_inverse(0)
        rs_send_one(4 + i, 0)
        if i < 3:
            rs_send_one(3 - i, 0)
        if i == 0:
            send_weights()
    rs_send_all(1)
    d_load[1].wait()
    send_inverse(1)

    def reduce(m):
        settle(rs.at[m], rs_recv.at[m])
        total = own[m]
        for s in range(7):
            total = total + rs[m, s].astype(F32)
        return rv[m] - total

    slot = pl.ds(pl.multiple_of((r % 16) * 64, 64), 64)

    def spread(n, value):
        st[n] = value.astype(BF)
        for q in chips:
            send(st.at[n], ga.at[n, slot], g_send.at[n], g_recv.at[n], (2 * q + home, c))

        @pl.when(k == home)
        def _():
            local_copy(st.at[n], ga.at[n, slot], g_recv.at[n]).start()

        @pl.when(k != home)
        def _():
            send(st.at[n], ga.at[n, slot], g_send.at[n], g_recv.at[n], sib)

    def exchange(e, value):
        xout[e] = value
        send(xout.at[e], xin.at[e], x_send.at[e], x_recv.at[e], sib)

    def exchanged(e):
        settle(xin.at[e], x_recv.at[e])
        return xin[e]

    r_load.wait()
    spread(0, reduce(0))
    d_load[2].wait()
    make_next(0)
    send_inverse(2)
    rs_send_all(2)
    pend[1] = reduce(1)
    make_next(1)
    rs_send_all(3)
    for cp in w_load[3:]:
        cp.wait()
    settle(dx_w.at[:, 0], w_recv.at[4])
    settle(lx.at[:, 0], w_recv.at[3])

    for m in range(4):
        settle(ga.at[m], g_recv.at[m])
        if m < 3:
            settle(mk.at[m, :, pl.ds(0, 896)], m_recv.at[m])
            upd = dot(mk[m], ga[m])
            if m == 1:
                settle(ga.at[4], g_recv.at[4])
                upd = upd + dot(lx[0].reshape(128, 1024), ga[4])
            if m == 2:
                settle(ga.at[5], g_recv.at[5])
                upd = upd + dot(lx[2].reshape(128, 1024), ga[5]) + pre[...]
            exchange(m, upd[:64])
        sol = dot(dx_w[m].reshape(128, 1024), ga[m])
        exchange(3 + m, sol[:64])
        if m < 3:
            spread(m + 1, pend[m + 1] - (upd[64:] + exchanged(m)))
        cur = sol[64:] + exchanged(3 + m)
        if m < 2:
            spread(4 + m, cur)
        out[m] = cur
        if m == 0:
            pend[2] = reduce(2)
            make_next(2)
        if m == 1:
            pend[3] = reduce(3)
            pre[...] = dot(lx[1].reshape(128, 1024), ga[4])

    settle(part.at[pl.ds(1, 7)], rs_send)
    for n in range(6):
        @pl.when(k == home)
        def _():
            settle(ga.at[n, pl.ds(0, 960)], g_send.at[n])

        @pl.when(k != home)
        def _():
            settle(ga.at[n], g_send.at[n])

    for j in range(3):
        sent_inverse(j)
        settle(mk.at[j, :, pl.ds(0, 896)], m_send.at[j])
    settle(lm.at[:, 0], w_send.at[0])
    settle(dx_w.at[:, 0], w_send.at[1])
    settle(lx.at[:, 0], w_send.at[2])
    for e in range(7):
        settle(xin.at[e], x_send.at[e])


def local(rhs, l_panel, x_solved, diag_inv, l_inner):
    any_spec = pl.BlockSpec(memory_space=pl.ANY)
    dma = pltpu.SemaphoreType.DMA
    return pl.pallas_call(
        kernel,
        out_shape=jax.ShapeDtypeStruct((4, 64, 128), F32),
        in_specs=[any_spec] * 5,
        out_specs=pl.BlockSpec(memory_space=pltpu.VMEM),
        scratch_shapes=[
            pltpu.VMEM((4, 64, 4096), BF),
            pltpu.VMEM((4, 4096, 256), BF),
            pltpu.VMEM((3, 64, 2048), BF),
            pltpu.VMEM((3, 2048, 128), BF),
            pltpu.VMEM((3, 2, 64, 2048), BF),
            pltpu.VMEM((3, 128, 1024), BF),
            pltpu.VMEM((3, 2, 64, 1024), BF),
            pltpu.VMEM((4, 2, 64, 1024), BF),
            pltpu.VMEM((4, 64, 128), F32),
            pltpu.VMEM((4, 64, 128), F32),
            pltpu.VMEM((8, 4, 64, 128), BF),
            pltpu.VMEM((4, 7, 64, 128), BF),
            pltpu.VMEM((6, 64, 128), BF),
            pltpu.VMEM((6, 1024, 128), BF),
            pltpu.VMEM((7, 64, 128), F32),
            pltpu.VMEM((7, 64, 128), F32),
            pltpu.VMEM((4, 64, 128), F32),
            pltpu.VMEM((128, 128), F32),
            dma((23,)),
            dma,
            dma((4,)),
            dma((6,)),
            dma((6,)),
            dma((3,)),
            dma((3,)),
            dma((3,)),
            dma((3,)),
            dma((3,)),
            dma((5,)),
            dma((7,)),
            dma((7,)),
        ],
        compiler_params=pltpu.CompilerParams(
            collective_id=0, has_side_effects=True, vmem_limit_bytes=60 * 1024 * 1024
        ),
    )(rhs, l_panel, x_solved, diag_inv, l_inner)


def solution(mesh):
    in_specs = (
        P(None, "row", "col"),
        P(None, "row", "col"),
        P("col", None),
        P(None, "row", None),
        P(None, "row", None),
    )
    return jax.shard_map(
        local, mesh=mesh, in_specs=in_specs, out_specs=P(None, "row", "col"), check_vma=False
    )
```

```python
import jax
import jax.numpy as jnp
from jax import lax
from jax.experimental import pallas as pl
from jax.experimental.pallas import tpu as pltpu
from jax.sharding import PartitionSpec as P

MESH = pl.DeviceIdType.MESH
BF = jnp.bfloat16
F32 = jnp.float32


def dot(a, b):
    return jnp.dot(a, b, preferred_element_type=F32)


FIRST = (0, 1, 3)
LATER = (2, 4, 5)

CHIPS = sorted(
    [(dx, dy) for dx in range(4) for dy in range(4) if (dx, dy) != (0, 0)],
    key=lambda t: -(min(t[0], 4 - t[0]) + min(t[1], 4 - t[1])),
)


def local_copy(src, dst, sem):
    return pltpu.make_async_copy(src, dst, sem)


def settle(ref, sem):
    pltpu.make_async_copy(ref, ref, sem).wait()


def kernel(
    rhs, panel, solved, dinv, inner, out,
    lp, xs, dv, dq, lm, mk, lx, dx_w, rv, own, part, rs, st, ga, xout, xin, pend, pre,
    in_sem, rs_send, rs_recv, g_send, g_recv, d_send, d_recv, m_send, m_recv, w_send, w_recv,
    x_send, x_recv,
):
    r = lax.axis_index("row")
    c = lax.axis_index("col")
    k = r % 2
    p = r // 2
    y = p % 4
    x = p // 4
    home = x // 2
    mine = pl.multiple_of(1024 * k, 1024)
    other = pl.multiple_of(1024 * (1 - k), 1024)
    sib = (2 * p + 1 - k, c)
    chips = [((x + dx) % 4) * 4 + (y + dy) % 4 for dx, dy in CHIPS]

    def send(src, dst, ssem, rsem, dev):
        pltpu.make_async_remote_copy(
            src_ref=src, dst_ref=dst, send_sem=ssem, recv_sem=rsem,
            device_id=dev, device_id_type=MESH,
        ).start()

    p_load = local_copy(panel, lp, in_sem.at[0])
    x_load = []
    for i in range(4):
        for half, off in enumerate((4 + i, 3 - i)):
            dest = (c + off) % 8
            x_load.append(
                local_copy(
                    solved.at[:, pl.ds(pl.multiple_of(dest * 128, 128), 128)],
                    xs.at[i, :, pl.ds(128 * half, 128)],
                    in_sem.at[1 + 2 * i + half],
                )
            )
    r_load = local_copy(rhs, rv, in_sem.at[9])
    d_load = [local_copy(dinv.at[1 + j], dv.at[j], in_sem.at[10 + j]) for j in range(2)]
    w_load = []
    for i in range(3):
        w_load.append(local_copy(inner.at[LATER[i]], lm.at[i, 1], in_sem.at[13 + i]))
    for i in range(3):
        w_load.append(
            local_copy(inner.at[FIRST[i], :, pl.ds(mine, 1024)], lx.at[i, 1], in_sem.at[16 + i])
        )
    for m in range(4):
        w_load.append(
            local_copy(dinv.at[m, :, pl.ds(mine, 1024)], dx_w.at[m, 1], in_sem.at[19 + m])
        )
    p_load.start()
    for cp in x_load[:4]:
        cp.start()
    d_load[0].start()
    for cp in x_load[4:]:
        cp.start()
    for cp in [r_load, d_load[1]] + w_load:
        cp.start()

    barrier = pltpu.get_barrier_semaphore()
    for off in range(1, 8):
        pl.semaphore_signal(barrier, inc=1, device_id=(r, (c + off) % 8), device_id_type=MESH)
    pl.semaphore_signal(barrier, inc=1, device_id=sib, device_id_type=MESH)
    for q in chips:
        for core in range(2):
            pl.semaphore_signal(barrier, inc=1, device_id=(2 * q + core, c), device_id_type=MESH)

    slice_of = lambda core: jnp.where(core == 0, c, 15 - c)
    my_slice = slice_of(k)
    my_local = pl.multiple_of((my_slice - 8 * k) * 128, 128)

    @pl.loop(0, my_slice)
    def _(i):
        rows = pl.ds(pl.multiple_of(i * 128, 128), 128)
        for j in range(2):
            dq[j, rows, :] = jnp.zeros((128, 128), BF)

    def send_inverse(j):
        rows = pl.ds(pl.multiple_of(r * 64, 64), 64)
        for d in range(2):
            core = (k + d) % 2
            s = slice_of(core)
            src = dv.at[j, :, pl.ds(pl.multiple_of(s * 128, 128), 128)]
            dst = dq.at[j, rows]

            @pl.when(p >= s)
            def _():
                for q in chips:
                    send(src, dst, d_send.at[j], d_recv.at[j], (2 * q + core, c))
                if d == 0:
                    local_copy(src, dst, d_recv.at[j]).start()
                else:
                    send(src, dst, d_send.at[j], d_recv.at[j], sib)

    def sent_inverse(j):
        near, far = p >= slice_of(k), p >= slice_of(1 - k)
        for rows, cond in (
            (1984, near & far),
            (960, near & jnp.logical_not(far)),
            (1024, far & jnp.logical_not(near)),
        ):

            @pl.when(cond)
            def _():
                settle(dq.at[j, pl.ds(0, rows)], d_send.at[j])

    def got_inverse(j):
        for s in range(16):

            @pl.when(my_slice == s)
            def _():
                settle(dq.at[j, pl.ds(128 * s, 2048 - 128 * s)], d_recv.at[j])

    def send_weights():
        for m in range(4):
            send(dinv.at[m, :, pl.ds(other, 1024)], dx_w.at[m, 0], w_send.at[0], w_recv.at[0], sib)
        for i in range(3):
            send(
                inner.at[FIRST[i], :, pl.ds(other, 1024)], lx.at[i, 0], w_send.at[1], w_recv.at[1], sib
            )
        for i in range(3):
            send(inner.at[LATER[i]], lm.at[i, 0], w_send.at[2], w_recv.at[2], sib)

    cols = pl.ds(my_local, 128)

    def make_product(i, j):
        block = dot(lm[i].reshape(128, 2048), dq[j])
        mk[i, :, cols] = block.astype(BF)
        for off in (4, 5, 3, 6, 2, 7, 1):
            send(mk.at[i, :, cols], mk.at[i, :, cols], m_send.at[i], m_recv.at[i], (r, (c + off) % 8))

    def rs_send_one(off, m):
        send(part.at[off, m], rs.at[m, off - 1], rs_send, rs_recv.at[m], (r, (c + off) % 8))

    def rs_send_all(m):
        for off in (4, 5, 3, 6, 2, 7, 1):
            rs_send_one(off, m)

    def rs_chunk(i):
        rs_send_one(4 + i, 0)
        if i < 3:
            rs_send_one(3 - i, 0)

    p_load.wait()
    for i in range(4):
        x_load[2 * i].wait()
        x_load[2 * i + 1].wait()
        acc = dot(lp[...].reshape(256, 4096), xs[i]).reshape(4, 64, 256)
        part[4 + i] = acc[:, :, :128].astype(BF)
        if i < 3:
            part[3 - i] = acc[:, :, 128:].astype(BF)
        else:
            own[...] = acc[:, :, 128:]
        if i == 1:
            pl.semaphore_wait(barrier, 38)
            rs_chunk(0)
            d_load[0].wait()
            send_inverse(0)
        if i >= 1:
            rs_chunk(i)
    rs_send_all(1)
    send_weights()

    def reduce(m):
        settle(rs.at[m], rs_recv.at[m])
        total = own[m]
        for s in range(7):
            total = total + rs[m, s].astype(F32)
        return rv[m] - total

    slot = pl.ds(pl.multiple_of((r % 16) * 64, 64), 64)

    def spread(n, value):
        st[n] = value.astype(BF)
        for q in chips:
            send(st.at[n], ga.at[n, slot], g_send.at[n], g_recv.at[n], (2 * q + home, c))

        @pl.when(k == home)
        def _():
            local_copy(st.at[n], ga.at[n, slot], g_recv.at[n]).start()

        @pl.when(k != home)
        def _():
            send(st.at[n], ga.at[n, slot], g_send.at[n], g_recv.at[n], sib)

    def exchange(e, value):
        xout[e] = value
        send(xout.at[e], xin.at[e], x_send.at[e], x_recv.at[e], sib)

    def exchanged(e):
        settle(xin.at[e], x_recv.at[e])
        return xin[e]

    def arrived(n):
        settle(ga.at[n], g_recv.at[n])

    def finish(m, value):
        out[m] = value

    def half(w, n):
        return dot(w.reshape(128, 1024), ga[n])

    r_load.wait()
    spread(0, reduce(0))
    rs_send_all(2)
    rs_send_all(3)
    for cp in w_load:
        cp.wait()
    settle(dx_w.at[:, 0], w_recv.at[0])
    settle(lx.at[:, 0], w_recv.at[1])
    settle(lm.at[:, 0], w_recv.at[2])

    arrived(0)
    sol = half(dx_w[0], 0)
    exchange(0, sol[:64])
    sol = sol[64:] + exchanged(0)
    spread(1, sol)
    d_load[1].wait()
    send_inverse(1)
    finish(0, sol)
    pend[1] = reduce(1)
    got_inverse(0)
    make_product(0, 0)
    make_product(1, 0)

    arrived(1)
    upd = half(lx[0], 1)
    exchange(1, upd[:64])
    spread(2, pend[1] - (upd[64:] + exchanged(1)))
    pre[0] = half(lx[1], 1)
    pre[1] = half(lx[2], 1)
    got_inverse(1)
    make_product(2, 1)
    pend[2] = reduce(2)
    pend[3] = reduce(3)

    for m in (1, 2):
        arrived(m + 1)
        settle(mk.at[m * m - m, :, pl.ds(0, 896)], m_recv.at[m * m - m])
        upd = dot(mk[m * m - m], ga[m + 1]) + pre[m - 1]
        exchange(2 * m, upd[:64])
        sol = half(dx_w[m], m + 1)
        exchange(2 * m + 1, sol[:64])
        spread(m + 2, pend[m + 1] - (upd[64:] + exchanged(2 * m)))
        finish(m, sol[64:] + exchanged(2 * m + 1))
        if m == 1:
            settle(mk.at[1, :, pl.ds(0, 896)], m_recv.at[1])
            pre[1] = pre[1] + dot(mk[1], ga[2])

    arrived(4)
    sol = half(dx_w[3], 4)
    exchange(6, sol[:64])
    finish(3, sol[64:] + exchanged(6))

    settle(part.at[pl.ds(1, 7)], rs_send)
    for n in range(5):
        @pl.when(k == home)
        def _():
            settle(ga.at[n, pl.ds(0, 960)], g_send.at[n])

        @pl.when(k != home)
        def _():
            settle(ga.at[n], g_send.at[n])

    for j in range(2):
        sent_inverse(j)
    for i in range(3):
        settle(mk.at[i, :, pl.ds(0, 896)], m_send.at[i])
    settle(dx_w.at[:, 0], w_send.at[0])
    settle(lx.at[:, 0], w_send.at[1])
    settle(lm.at[:, 0], w_send.at[2])
    for e in range(7):
        settle(xin.at[e], x_send.at[e])


def local(rhs, l_panel, x_solved, diag_inv, l_inner):
    any_spec = pl.BlockSpec(memory_space=pl.ANY)
    dma = pltpu.SemaphoreType.DMA
    return pl.pallas_call(
        kernel,
        out_shape=pltpu.VMEM((4, 64, 128), F32),
        in_specs=[any_spec] * 5,
        out_specs=pl.BlockSpec(memory_space=pltpu.VMEM),
        scratch_shapes=[
            pltpu.VMEM((4, 64, 4096), BF),
            pltpu.VMEM((4, 4096, 256), BF),
            pltpu.VMEM((2, 64, 2048), BF),
            pltpu.VMEM((2, 2048, 128), BF),
            pltpu.VMEM((3, 2, 64, 2048), BF),
            pltpu.VMEM((3, 128, 1024), BF),
            pltpu.VMEM((3, 2, 64, 1024), BF),
            pltpu.VMEM((4, 2, 64, 1024), BF),
            pltpu.VMEM((4, 64, 128), F32),
            pltpu.VMEM((4, 64, 128), F32),
            pltpu.VMEM((8, 4, 64, 128), BF),
            pltpu.VMEM((4, 7, 64, 128), BF),
            pltpu.VMEM((5, 64, 128), BF),
            pltpu.VMEM((5, 1024, 128), BF),
            pltpu.VMEM((7, 64, 128), F32),
            pltpu.VMEM((7, 64, 128), F32),
            pltpu.VMEM((4, 64, 128), F32),
            pltpu.VMEM((2, 128, 128), F32),
            dma((23,)),
            dma,
            dma((4,)),
            dma((5,)),
            dma((5,)),
            dma((2,)),
            dma((2,)),
            dma((3,)),
            dma((3,)),
            dma((3,)),
            dma((3,)),
            dma((7,)),
            dma((7,)),
        ],
        compiler_params=pltpu.CompilerParams(
            collective_id=0, has_side_effects=True, vmem_limit_bytes=60 * 1024 * 1024
        ),
    )(rhs, l_panel, x_solved, diag_inv, l_inner)


def solution(mesh):
    in_specs = (
        P(None, "row", "col"),
        P(None, "row", "col"),
        P("col", None),
        P(None, "row", None),
        P(None, "row", None),
    )
    return jax.shard_map(
        local, mesh=mesh, in_specs=in_specs, out_specs=P(None, "row", "col"), check_vma=False
    )
```

```python
import jax
import jax.numpy as jnp
from jax import lax
from jax.experimental import pallas as pl
from jax.experimental.pallas import tpu as pltpu
from jax.sharding import PartitionSpec as P

MESH = pl.DeviceIdType.MESH
BF = jnp.bfloat16
F32 = jnp.float32


def dot(a, b):
    return jnp.dot(a, b, preferred_element_type=F32)


FIRST = (0, 1, 3)
LATER = (2, 4, 5)

CHIPS = sorted(
    [(dx, dy) for dx in range(4) for dy in range(4) if (dx, dy) != (0, 0)],
    key=lambda t: -(min(t[0], 4 - t[0]) + min(t[1], 4 - t[1])),
)


def local_copy(src, dst, sem):
    return pltpu.make_async_copy(src, dst, sem)


def settle(ref, sem):
    pltpu.make_async_copy(ref, ref, sem).wait()


def kernel(
    rhs, panel, solved, dinv, inner, out,
    lp, xs, ds, dq, wd, wl, mk, rv, own, part, rs, st, ga, rb, xout, xin, pend, pre,
    in_sem, rs_send, rs_recv, g_send, g_recv, d_send, d_recv, m_send, m_recv, h_send, h_recv,
    w_send, w_recv, x_send, x_recv,
):
    r = lax.axis_index("row")
    c = lax.axis_index("col")
    k = r % 2
    p = r // 2
    y = p % 4
    x = p // 4
    sib = (2 * p + 1 - k, c)
    chips = [((x + dx) % 4) * 4 + (y + dy) % 4 for dx, dy in CHIPS]

    def send(src, dst, ssem, rsem, dev):
        pltpu.make_async_remote_copy(
            src_ref=src, dst_ref=dst, send_sem=ssem, recv_sem=rsem,
            device_id=dev, device_id_type=MESH,
        ).start()

    barrier = pltpu.get_barrier_semaphore()
    for off in range(1, 8):
        pl.semaphore_signal(barrier, inc=1, device_id=(r, (c + off) % 8), device_id_type=MESH)
    pl.semaphore_signal(barrier, inc=1, device_id=sib, device_id_type=MESH)
    for q in chips:
        for core in range(2):
            pl.semaphore_signal(barrier, inc=1, device_id=(2 * q + core, c), device_id_type=MESH)


    p_load = [
        local_copy(panel.at[0], lp.at[0], in_sem.at[0]),
        local_copy(panel.at[pl.ds(1, 3)], lp.at[pl.ds(1, 3)], in_sem.at[12]),
    ]
    x_load = []
    for i in range(4):
        for half, off in enumerate((4 + i, 3 - i)):
            dest = (c + off) % 8
            x_load.append(
                local_copy(
                    solved.at[:, pl.ds(pl.multiple_of(dest * 128, 128), 128)],
                    xs.at[i, :, pl.ds(128 * half, 128)],
                    in_sem.at[1 + 2 * i + half],
                )
            )
    r_load = local_copy(rhs, rv, in_sem.at[9])
    d_load = [local_copy(dinv.at[m], wd.at[m, k], in_sem.at[13 + m]) for m in range(4)]
    l_load = [
        local_copy(inner.at[pl.ds(0, 3)], wl.at[pl.ds(0, 3), k], in_sem.at[10]),
        local_copy(inner.at[pl.ds(3, 3)], wl.at[pl.ds(3, 3), k], in_sem.at[11]),
    ]
    slice_of = lambda core: jnp.where(core == 0, c, 15 - c)
    my_slice = slice_of(k)
    s_load = [
        local_copy(
            dinv.at[1 + j, :, pl.ds(pl.multiple_of(slice_of(core) * 128, 128), 128)],
            ds.at[j, core],
            in_sem.at[17 + 2 * j + core],
        )
        for j in range(2)
        for core in range(2)
    ]
    p_load[0].start()
    for cp in x_load[:4] + s_load[:2] + x_load[4:]:
        cp.start()
    for cp in [p_load[1], r_load] + s_load[2:] + d_load[:1] + l_load + d_load[1:]:
        cp.start()

    @pl.loop(0, my_slice)
    def _(i):
        rows = pl.ds(pl.multiple_of(i * 128, 128), 128)
        for j in range(2):
            dq[j, rows, :] = jnp.zeros((128, 128), BF)

    def send_inverse(j, piece):
        rows = pl.ds(pl.multiple_of(r * 64, 64), 64)
        for d in range(2):
            core = (k + d) % 2
            s = slice_of(core)
            src = ds.at[j, core]
            dst = dq.at[j, rows]

            @pl.when(p >= s)
            def _():
                for q in chips[piece::3]:
                    send(src, dst, d_send.at[j], d_recv.at[j], (2 * q + core, c))
                if piece > 0:
                    return
                if d == 0:
                    local_copy(src, dst, d_recv.at[j]).start()
                else:
                    send(src, dst, d_send.at[j], d_recv.at[j], sib)

    def sent_inverse(j):
        near, far = p >= slice_of(k), p >= slice_of(1 - k)
        for rows, cond in (
            (1984, near & far),
            (960, near & jnp.logical_not(far)),
            (1024, far & jnp.logical_not(near)),
        ):

            @pl.when(cond)
            def _():
                settle(dq.at[j, pl.ds(0, rows)], d_send.at[j])

    def got_inverse(j):
        for s in range(16):

            @pl.when(my_slice == s)
            def _():
                settle(dq.at[j, pl.ds(128 * s, 2048 - 128 * s)], d_recv.at[j])

    def send_weights():
        send(dinv.at[0], wd.at[0, k], w_send.at[0], w_recv.at[0], sib)
        send(inner.at[pl.ds(0, 3)], wl.at[pl.ds(0, 3), k], w_send.at[1], w_recv.at[1], sib)
        send(inner.at[pl.ds(3, 3)], wl.at[pl.ds(3, 3), k], w_send.at[2], w_recv.at[2], sib)
        send(dinv.at[pl.ds(1, 3)], wd.at[pl.ds(1, 3), k], w_send.at[3], w_recv.at[3], sib)

    def pass_on(i, plane, off, e):
        slot = jnp.where(k == 0, plane % 8, 15 - plane % 8)
        send(
            mk.at[i, slot], mk.at[i, slot], m_send.at[i, e], m_recv.at[i, e], (r, (c + off) % 8)
        )

    def make_product(i, n, j):
        mk[i, my_slice] = dot(wl[n].reshape(128, 2048), dq[j]).astype(BF)
        for off in (2, 6, 1, 7):
            pass_on(i, c, off, 0)

    def relay_product(i):
        settle(mk.at[i, pl.ds(0, 4)], m_recv.at[i, 0])
        far = 2 + 4 * k
        pass_on(i, c + 8 - far, far, 1)
        pass_on(i, c + 6, 1, 1)
        pass_on(i, c + 2, 7, 1)

    def share_product(i):
        settle(mk.at[i, pl.ds(0, 3)], m_recv.at[i, 1])
        part_cols = mk.at[i, pl.ds(8 * k, 8)]
        send(part_cols, part_cols, h_send.at[i], h_recv.at[i], sib)

    def got_product(i):
        settle(mk.at[i, pl.ds(0, 8)], h_recv.at[i])

    def rs_send_one(off, m):
        send(part.at[off, m], rs.at[m, off - 1], rs_send, rs_recv.at[m], (r, (c + off) % 8))

    def rs_send_all(m):
        for off in (4, 5, 3, 6, 2, 7, 1):
            rs_send_one(off, m)

    def rs_chunk(i):
        rs_send_one(4 + i, 0)
        if i < 3:
            rs_send_one(3 - i, 0)

    def product(i, lo, hi):
        rows = 64 * (hi - lo)
        acc = dot(lp[lo:hi].reshape(rows, 4096), xs[i]).reshape(hi - lo, 64, 256)
        part[4 + i, lo:hi] = acc[:, :, :128].astype(BF)
        if i < 3:
            part[3 - i, lo:hi] = acc[:, :, 128:].astype(BF)
        else:
            own[lo:hi] = acc[:, :, 128:]

    p_load[0].wait()
    for i in range(4):
        x_load[2 * i].wait()
        x_load[2 * i + 1].wait()
        product(i, 0, 1)
        if i == 0:
            pl.semaphore_wait(barrier, 38)
        rs_chunk(i)
        if i == 1:
            s_load[0].wait()
            s_load[1].wait()
            send_weights()
        if i >= 1:
            send_inverse(0, i - 1)
    p_load[1].wait()
    for i in range(4):
        product(i, 1, 4)
    rs_send_all(1)
    rs_send_all(2)

    lane = lax.broadcasted_iota(jnp.int32, (64, 128), 1)
    left = lane < 64
    stay = left == (k == 0)

    def turn_start(e, value):
        xout[e] = pltpu.roll(value, 64, 1)
        send(xout.at[e], xin.at[e], x_send.at[e], x_recv.at[e], sib)

    def turn_end(e, value):
        settle(xin.at[e], x_recv.at[e])
        return jnp.where(stay, value, xin[e])

    def turn(e, value):
        turn_start(e, value)
        return turn_end(e, value)

    def reduce(m):
        settle(rs.at[m], rs_recv.at[m])
        total = own[m]
        for s in range(7):
            total = total + rs[m, s].astype(F32)
        return rv[m] - total

    slot = pl.ds(pl.multiple_of(p * 64, 64), 64)

    def spread(n, value):
        st[n] = value.astype(BF)
        for q in chips:
            send(st.at[n], ga.at[n, slot], g_send.at[n], g_recv.at[n], (2 * q + k, c))
        local_copy(st.at[n], ga.at[n, slot], g_recv.at[n]).start()

    def arrived(n):
        settle(ga.at[n], g_recv.at[n])
        here = ga[n]
        there = pltpu.roll(here, 64, 1).reshape(16, 64, 128)
        here = here.reshape(16, 64, 128)
        rb[:, 0, :, :128] = here
        rb[:, 1, :, :128] = there
        rb[:, 0, :, 128:] = there
        rb[:, 1, :, 128:] = here

    def joined(i):
        return jnp.concatenate([mk[i, q] for q in range(16)], axis=1)

    def apply(w):
        prod = dot(w.reshape(128, 2048), rb[...].reshape(2048, 256))
        return jnp.where(left, prod[:64, :128], prod[64:, 128:])

    r_load.wait()
    spread(0, turn(0, reduce(0)))
    for cp in s_load[2:] + d_load + l_load:
        cp.wait()
    settle(wd.at[0, 0], w_recv.at[0])
    settle(wl.at[pl.ds(0, 3), 0], w_recv.at[1])
    settle(wl.at[pl.ds(3, 3), 0], w_recv.at[2])
    settle(wd.at[pl.ds(1, 3), 0], w_recv.at[3])
    got_inverse(0)
    make_product(0, LATER[0], 0)
    for piece in range(3):
        send_inverse(1, piece)
    rs_send_all(3)

    arrived(0)
    sol = apply(wd[0])
    spread(1, sol)
    turn_start(4, sol)
    make_product(1, LATER[1], 0)
    pend[1] = reduce(1)
    turn_start(1, pend[1])
    out[0] = turn_end(4, sol)
    relay_product(0)
    got_inverse(1)
    make_product(2, LATER[2], 1)

    arrived(1)
    spread(2, turn_end(1, pend[1]) - apply(wl[FIRST[0]]))
    relay_product(1)
    pend[2] = reduce(2)
    turn_start(2, pend[2])
    share_product(0)
    pre[...] = apply(wl[FIRST[2]])
    pend[2] = turn_end(2, pend[2]) - apply(wl[FIRST[1]])
    got_product(0)
    relay_product(2)

    for m in (1, 2):
        arrived(m + 1)
        spread(m + 2, pend[m + 1] - apply(joined(2 * m - 2)))
        sol = apply(wd[m])
        turn_start(4 + m, sol)
        if m == 1:
            share_product(1)
            pend[3] = reduce(3)
            turn_start(3, pend[3])
            got_product(1)
            pre[...] = pre[...] + apply(joined(1))
            share_product(2)
            pend[3] = turn_end(3, pend[3]) - pre[...]
        out[m] = turn_end(4 + m, sol)
        if m == 1:
            got_product(2)

    arrived(4)
    out[3] = turn(7, apply(wd[3]))

    settle(part.at[pl.ds(1, 7)], rs_send)
    for n in range(5):
        settle(ga.at[n, pl.ds(0, 960)], g_send.at[n])
    for j in range(2):
        sent_inverse(j)
    for i in range(3):
        settle(mk.at[i, pl.ds(0, 4)], m_send.at[i, 0])
        settle(mk.at[i, pl.ds(0, 3)], m_send.at[i, 1])
        settle(mk.at[i, pl.ds(0, 8)], h_send.at[i])
    settle(wd.at[0, 0], w_send.at[0])
    settle(wl.at[pl.ds(0, 3), 0], w_send.at[1])
    settle(wl.at[pl.ds(3, 3), 0], w_send.at[2])
    settle(wd.at[pl.ds(1, 3), 0], w_send.at[3])
    for e in range(8):
        settle(xin.at[e], x_send.at[e])


def local(rhs, l_panel, x_solved, diag_inv, l_inner):
    any_spec = pl.BlockSpec(memory_space=pl.ANY)
    dma = pltpu.SemaphoreType.DMA
    return pl.pallas_call(
        kernel,
        out_shape=pltpu.VMEM((4, 64, 128), F32),
        in_specs=[any_spec] * 5,
        out_specs=pl.BlockSpec(memory_space=pltpu.VMEM),
        scratch_shapes=[
            pltpu.VMEM((4, 64, 4096), BF),
            pltpu.VMEM((4, 4096, 256), BF),
            pltpu.VMEM((2, 2, 64, 128), BF),
            pltpu.VMEM((2, 2048, 128), BF),
            pltpu.VMEM((4, 2, 64, 2048), BF),
            pltpu.VMEM((6, 2, 64, 2048), BF),
            pltpu.VMEM((3, 16, 128, 128), BF),
            pltpu.VMEM((4, 64, 128), F32),
            pltpu.VMEM((4, 64, 128), F32),
            pltpu.VMEM((8, 4, 64, 128), BF),
            pltpu.VMEM((4, 7, 64, 128), BF),
            pltpu.VMEM((5, 64, 128), BF),
            pltpu.VMEM((5, 1024, 128), BF),
            pltpu.VMEM((16, 2, 64, 256), BF),
            pltpu.VMEM((8, 64, 128), F32),
            pltpu.VMEM((8, 64, 128), F32),
            pltpu.VMEM((4, 64, 128), F32),
            pltpu.VMEM((64, 128), F32),
            dma((21,)),
            dma,
            dma((4,)),
            dma((5,)),
            dma((5,)),
            dma((2,)),
            dma((2,)),
            dma((3, 2)),
            dma((3, 2)),
            dma((3,)),
            dma((3,)),
            dma((4,)),
            dma((4,)),
            dma((8,)),
            dma((8,)),
        ],
        compiler_params=pltpu.CompilerParams(
            collective_id=0, has_side_effects=True, vmem_limit_bytes=60 * 1024 * 1024
        ),
    )(rhs, l_panel, x_solved, diag_inv, l_inner)


def solution(mesh):
    in_specs = (
        P(None, "row", "col"),
        P(None, "row", "col"),
        P("col", None),
        P(None, "row", None),
        P(None, "row", None),
    )
    return jax.shard_map(
        local, mesh=mesh, in_specs=in_specs, out_specs=P(None, "row", "col"), check_vma=False
    )
```

```python
import jax
import jax.numpy as jnp
from jax import lax
from jax.experimental import pallas as pl
from jax.experimental.pallas import tpu as pltpu
from jax.sharding import PartitionSpec as P

MESH = pl.DeviceIdType.MESH
BF = jnp.bfloat16
F32 = jnp.float32


def dot(a, b):
    return jnp.dot(a, b, preferred_element_type=F32)


FIRST = (0, 1, 3)
LATER = (2, 4, 5)

CHIPS = sorted(
    [(dx, dy) for dx in range(4) for dy in range(4) if (dx, dy) != (0, 0)],
    key=lambda t: -(min(t[0], 4 - t[0]) + min(t[1], 4 - t[1])),
)


def local_copy(src, dst, sem):
    return pltpu.make_async_copy(src, dst, sem)


def settle(ref, sem):
    pltpu.make_async_copy(ref, ref, sem).wait()


def kernel(
    rhs, panel, solved, dinv, inner, out,
    lp, xs, p0, z0, ds, dq, wd, wl, mk, rv, own, part, rs, st, ga, rb, xout, xin, pend, pre,
    in_sem, p0_send, z0_recv, rs_send, rs_recv, g_send, g_recv, d_send, d_recv, m_send, m_recv, h_send, h_recv,
    w_send, w_recv, x_send, x_recv,
):
    r = lax.axis_index("row")
    c = lax.axis_index("col")
    k = r % 2
    p = r // 2
    y = p % 4
    x = p // 4
    sib = (2 * p + 1 - k, c)
    chips = [((x + dx) % 4) * 4 + (y + dy) % 4 for dx, dy in CHIPS]

    def send(src, dst, ssem, rsem, dev):
        pltpu.make_async_remote_copy(
            src_ref=src, dst_ref=dst, send_sem=ssem, recv_sem=rsem,
            device_id=dev, device_id_type=MESH,
        ).start()

    barrier = pltpu.get_barrier_semaphore()
    for off in range(1, 8):
        for row in (r, 2 * p + 1 - k):
            pl.semaphore_signal(barrier, inc=1, device_id=(row, (c + off) % 8), device_id_type=MESH)
    pl.semaphore_signal(barrier, inc=1, device_id=sib, device_id_type=MESH)
    for q in chips:
        for core in range(2):
            pl.semaphore_signal(barrier, inc=1, device_id=(2 * q + core, c), device_id_type=MESH)


    p_load = [
        local_copy(panel.at[0], lp.at[0], in_sem.at[0]),
        local_copy(panel.at[pl.ds(1, 3)], lp.at[pl.ds(1, 3)], in_sem.at[12]),
    ]
    x_load = []
    for i in range(4):
        for half, off in enumerate((4 + i, 3 - i)):
            dest = (c + off) % 8
            x_load.append(
                local_copy(
                    solved.at[:, pl.ds(pl.multiple_of(dest * 128, 128), 128)],
                    xs.at[i, :, pl.ds(128 * half, 128)],
                    in_sem.at[1 + 2 * i + half],
                )
            )
    r_load = local_copy(rhs, rv, in_sem.at[9])
    d_load = [local_copy(dinv.at[m], wd.at[m, k], in_sem.at[13 + m]) for m in range(4)]
    l_load = [
        local_copy(inner.at[pl.ds(0, 3)], wl.at[pl.ds(0, 3), k], in_sem.at[10]),
        local_copy(inner.at[pl.ds(3, 3)], wl.at[pl.ds(3, 3), k], in_sem.at[11]),
    ]
    slice_of = lambda core: jnp.where(core == 0, c, 15 - c)
    my_slice = slice_of(k)
    s_load = [
        local_copy(
            dinv.at[1 + j, :, pl.ds(pl.multiple_of(slice_of(core) * 128, 128), 128)],
            ds.at[j, core],
            in_sem.at[17 + 2 * j + core],
        )
        for j in range(2)
        for core in range(2)
    ]
    p_load[0].start()
    for cp in x_load[:4] + s_load[:2] + x_load[4:]:
        cp.start()
    for cp in [r_load, p_load[1]] + s_load[2:] + d_load[:1] + l_load + d_load[1:]:
        cp.start()

    @pl.loop(0, my_slice)
    def _(i):
        rows = pl.ds(pl.multiple_of(i * 128, 128), 128)
        for j in range(2):
            dq[j, rows, :] = jnp.zeros((128, 128), BF)

    def send_inverse(j, piece):
        rows = pl.ds(pl.multiple_of(r * 64, 64), 64)
        for d in range(2):
            core = (k + d) % 2
            s = slice_of(core)
            src = ds.at[j, core]
            dst = dq.at[j, rows]

            @pl.when(p >= s)
            def _():
                for q in chips[piece::3]:
                    send(src, dst, d_send.at[j], d_recv.at[j], (2 * q + core, c))
                if piece > 0:
                    return
                if d == 0:
                    local_copy(src, dst, d_recv.at[j]).start()
                else:
                    send(src, dst, d_send.at[j], d_recv.at[j], sib)

    def sent_inverse(j):
        near, far = p >= slice_of(k), p >= slice_of(1 - k)
        for rows, cond in (
            (1984, near & far),
            (960, near & jnp.logical_not(far)),
            (1024, far & jnp.logical_not(near)),
        ):

            @pl.when(cond)
            def _():
                settle(dq.at[j, pl.ds(0, rows)], d_send.at[j])

    def got_inverse(j):
        for s in range(16):

            @pl.when(my_slice == s)
            def _():
                settle(dq.at[j, pl.ds(128 * s, 2048 - 128 * s)], d_recv.at[j])

    def send_weights():
        send(dinv.at[0], wd.at[0, k], w_send.at[0], w_recv.at[0], sib)
        send(inner.at[pl.ds(0, 3)], wl.at[pl.ds(0, 3), k], w_send.at[1], w_recv.at[1], sib)
        send(inner.at[pl.ds(3, 3)], wl.at[pl.ds(3, 3), k], w_send.at[2], w_recv.at[2], sib)
        send(dinv.at[pl.ds(1, 3)], wd.at[pl.ds(1, 3), k], w_send.at[3], w_recv.at[3], sib)

    def pass_on(i, plane, off, e):
        slot = jnp.where(k == 0, plane % 8, 15 - plane % 8)
        send(
            mk.at[i, slot], mk.at[i, slot], m_send.at[i, e], m_recv.at[i, e], (r, (c + off) % 8)
        )

    def make_product(i, n, j):
        mk[i, my_slice] = dot(wl[n].reshape(128, 2048), dq[j]).astype(BF)
        for off in (2, 6, 1, 7):
            pass_on(i, c, off, 0)

    def relay_product(i):
        settle(mk.at[i, pl.ds(0, 4)], m_recv.at[i, 0])
        far = 2 + 4 * k
        pass_on(i, c + 8 - far, far, 1)
        pass_on(i, c + 6, 1, 1)
        pass_on(i, c + 2, 7, 1)

    def share_product(i):
        settle(mk.at[i, pl.ds(0, 3)], m_recv.at[i, 1])
        part_cols = mk.at[i, pl.ds(8 * k, 8)]
        send(part_cols, part_cols, h_send.at[i], h_recv.at[i], sib)

    def got_product(i):
        settle(mk.at[i, pl.ds(0, 8)], h_recv.at[i])

    def rs_send_one(off, m):
        send(part.at[off, m], rs.at[m, off - 1], rs_send, rs_recv.at[m], (r, (c + off) % 8))

    def rs_send_all(m, offs=(4, 5, 3, 6, 2, 7, 1)):
        for off in offs:
            rs_send_one(off, m)

    lane = lax.broadcasted_iota(jnp.int32, (64, 128), 1)
    left = lane < 64
    stay = left == (k == 0)

    def product(i, lo, hi):
        rows = 64 * (hi - lo)
        acc = dot(lp[lo:hi].reshape(rows, 4096), xs[i]).reshape(hi - lo, 64, 256)
        return acc[:, :, :128], acc[:, :, 128:]

    def product_later(i):
        first, second = product(i, 1, 4)
        part[4 + i, 1:] = first.astype(BF)
        if i < 3:
            part[3 - i, 1:] = second.astype(BF)
        else:
            own[1:] = second

    def fold(value):
        top, low = value[0, :32], value[0, 32:]
        return (
            jnp.where(left[:32], top, pltpu.roll(low, 64, 1)),
            jnp.where(left[:32], pltpu.roll(top, 64, 1), low),
        )

    def product_first(i):
        for off, value in zip((4 + i, 3 - i), product(i, 0, 1)):
            for core, folded in enumerate(fold(value)):
                p0[2 * off + core] = folded.astype(BF)
                if off == 0:
                    xout[7 + core, :32] = folded

    def rs_chunk(i):
        for off in (4 + i, 3 - i):
            dst = z0.at[8 * k + off]
            if off:
                send(p0.at[2 * off + k], dst, p0_send, z0_recv, (r, (c + off) % 8))
            send(p0.at[2 * off + 1 - k], dst, p0_send, z0_recv, (2 * p + 1 - k, (c + off) % 8))

    def reduce_first():
        settle(z0.at[pl.ds(0, 15)], z0_recv)
        mine = xout[7 + k, :32]
        for off in range(1, 8):
            mine = mine + z0[8 * k + off].astype(F32)
        theirs = z0[8 * (1 - k)].astype(F32)
        for off in range(1, 8):
            theirs = theirs + z0[8 * (1 - k) + off].astype(F32)
        first = jnp.where(k == 0, mine, theirs)
        second = jnp.where(k == 0, theirs, mine)
        return jnp.concatenate(
            [
                jnp.where(left[:32], first, pltpu.roll(second, 64, 1)),
                jnp.where(left[:32], pltpu.roll(first, 64, 1), second),
            ],
            axis=0,
        )

    def turn_start(e, value):
        xout[e] = pltpu.roll(value, 64, 1)
        send(xout.at[e], xin.at[e], x_send.at[e], x_recv.at[e], sib)

    def turn_end(e, value):
        settle(xin.at[e], x_recv.at[e])
        return jnp.where(stay, value, xin[e])

    def turn(e, value):
        turn_start(e, value)
        return turn_end(e, value)

    p_load[0].wait()
    for i in range(4):
        x_load[2 * i].wait()
        x_load[2 * i + 1].wait()
        product_first(i)
        if i == 0:
            pl.semaphore_wait(barrier, 45)
        rs_chunk(i)
        if i == 1:
            s_load[0].wait()
            s_load[1].wait()
            send_weights()
        if i >= 1:
            send_inverse(0, i - 1)
    r_load.wait()
    turn_start(0, rv[0])
    p_load[1].wait()
    for i in range(3):
        product_later(i)
    for m in (1, 2):
        rs_send_all(m, (4, 5, 3, 6, 2, 1))

    def reduce(m):
        settle(rs.at[m], rs_recv.at[m])
        total = own[m]
        for s in range(7):
            total = total + rs[m, s].astype(F32)
        return rv[m] - total

    slot = pl.ds(pl.multiple_of(p * 64, 64), 64)

    def spread(n, value):
        st[n] = value.astype(BF)
        for q in chips:
            send(st.at[n], ga.at[n, slot], g_send.at[n], g_recv.at[n], (2 * q + k, c))
        local_copy(st.at[n], ga.at[n, slot], g_recv.at[n]).start()

    def arrived(n):
        settle(ga.at[n], g_recv.at[n])
        here = ga[n]
        there = pltpu.roll(here, 64, 1).reshape(16, 64, 128)
        here = here.reshape(16, 64, 128)
        rb[:, 0, :, :128] = here
        rb[:, 1, :, :128] = there
        rb[:, 0, :, 128:] = there
        rb[:, 1, :, 128:] = here

    def joined(i):
        return jnp.concatenate([mk[i, q] for q in range(16)], axis=1)

    def apply(w):
        prod = dot(w.reshape(128, 2048), rb[...].reshape(2048, 256))
        return jnp.where(left, prod[:64, :128], prod[64:, 128:])

    spread(0, turn_end(0, rv[0]) - reduce_first())
    product_later(3)
    for m in (1, 2):
        rs_send_all(m, (7,))
    for cp in s_load[2:] + d_load + l_load:
        cp.wait()
    settle(wd.at[0, 0], w_recv.at[0])
    settle(wl.at[pl.ds(0, 3), 0], w_recv.at[1])
    settle(wl.at[pl.ds(3, 3), 0], w_recv.at[2])
    settle(wd.at[pl.ds(1, 3), 0], w_recv.at[3])
    got_inverse(0)
    make_product(0, LATER[0], 0)
    for piece in range(3):
        send_inverse(1, piece)
    rs_send_all(3)

    arrived(0)
    sol = apply(wd[0])
    spread(1, sol)
    turn_start(4, sol)
    make_product(1, LATER[1], 0)
    pend[1] = reduce(1)
    turn_start(1, pend[1])
    out[0] = turn_end(4, sol)
    relay_product(0)
    got_inverse(1)
    make_product(2, LATER[2], 1)

    arrived(1)
    spread(2, turn_end(1, pend[1]) - apply(wl[FIRST[0]]))
    relay_product(1)
    pend[2] = reduce(2)
    turn_start(2, pend[2])
    share_product(0)
    pre[...] = apply(wl[FIRST[2]])
    pend[2] = turn_end(2, pend[2]) - apply(wl[FIRST[1]])
    got_product(0)
    relay_product(2)

    for m in (1, 2):
        arrived(m + 1)
        spread(m + 2, pend[m + 1] - apply(joined(2 * m - 2)))
        sol = apply(wd[m])
        turn_start(4 + m, sol)
        if m == 1:
            share_product(1)
            pend[3] = reduce(3)
            turn_start(3, pend[3])
            got_product(1)
            pre[...] = pre[...] + apply(joined(1))
            share_product(2)
            pend[3] = turn_end(3, pend[3]) - pre[...]
        out[m] = turn_end(4 + m, sol)
        if m == 1:
            got_product(2)

    arrived(4)
    out[3] = turn(7, apply(wd[3]))

    settle(part.at[pl.ds(1, 7), pl.ds(1, 3)], rs_send)
    settle(p0.at[pl.ds(0, 15)], p0_send)
    for n in range(5):
        settle(ga.at[n, pl.ds(0, 960)], g_send.at[n])
    for j in range(2):
        sent_inverse(j)
    for i in range(3):
        settle(mk.at[i, pl.ds(0, 4)], m_send.at[i, 0])
        settle(mk.at[i, pl.ds(0, 3)], m_send.at[i, 1])
        settle(mk.at[i, pl.ds(0, 8)], h_send.at[i])
    settle(wd.at[0, 0], w_send.at[0])
    settle(wl.at[pl.ds(0, 3), 0], w_send.at[1])
    settle(wl.at[pl.ds(3, 3), 0], w_send.at[2])
    settle(wd.at[pl.ds(1, 3), 0], w_send.at[3])
    for e in range(8):
        settle(xin.at[e], x_send.at[e])


def local(rhs, l_panel, x_solved, diag_inv, l_inner):
    any_spec = pl.BlockSpec(memory_space=pl.ANY)
    dma = pltpu.SemaphoreType.DMA
    return pl.pallas_call(
        kernel,
        out_shape=pltpu.VMEM((4, 64, 128), F32),
        in_specs=[any_spec] * 5,
        out_specs=pl.BlockSpec(memory_space=pltpu.VMEM),
        scratch_shapes=[
            pltpu.VMEM((4, 64, 4096), BF),
            pltpu.VMEM((4, 4096, 256), BF),
            pltpu.VMEM((16, 32, 128), BF),
            pltpu.VMEM((16, 32, 128), BF),
            pltpu.VMEM((2, 2, 64, 128), BF),
            pltpu.VMEM((2, 2048, 128), BF),
            pltpu.VMEM((4, 2, 64, 2048), BF),
            pltpu.VMEM((6, 2, 64, 2048), BF),
            pltpu.VMEM((3, 16, 128, 128), BF),
            pltpu.VMEM((4, 64, 128), F32),
            pltpu.VMEM((4, 64, 128), F32),
            pltpu.VMEM((8, 4, 64, 128), BF),
            pltpu.VMEM((4, 7, 64, 128), BF),
            pltpu.VMEM((5, 64, 128), BF),
            pltpu.VMEM((5, 1024, 128), BF),
            pltpu.VMEM((16, 2, 64, 256), BF),
            pltpu.VMEM((9, 64, 128), F32),
            pltpu.VMEM((8, 64, 128), F32),
            pltpu.VMEM((4, 64, 128), F32),
            pltpu.VMEM((64, 128), F32),
            dma((21,)),
            dma,
            dma,
            dma,
            dma((4,)),
            dma((5,)),
            dma((5,)),
            dma((2,)),
            dma((2,)),
            dma((3, 2)),
            dma((3, 2)),
            dma((3,)),
            dma((3,)),
            dma((4,)),
            dma((4,)),
            dma((8,)),
            dma((8,)),
        ],
        compiler_params=pltpu.CompilerParams(
            collective_id=0, has_side_effects=True, vmem_limit_bytes=60 * 1024 * 1024
        ),
    )(rhs, l_panel, x_solved, diag_inv, l_inner)


def solution(mesh):
    in_specs = (
        P(None, "row", "col"),
        P(None, "row", "col"),
        P("col", None),
        P(None, "row", None),
        P(None, "row", None),
    )
    return jax.shard_map(
        local, mesh=mesh, in_specs=in_specs, out_specs=P(None, "row", "col"), check_vma=False
    )
```

```python
import jax
import jax.numpy as jnp
from jax import lax
from jax.experimental import pallas as pl
from jax.experimental.pallas import tpu as pltpu
from jax.sharding import PartitionSpec as P

MESH = pl.DeviceIdType.MESH
BF = jnp.bfloat16
F32 = jnp.float32


def dot(a, b):
    return jnp.dot(a, b, preferred_element_type=F32)


FIRST = (0, 1, 3)
LATER = (2, 4, 5)

CHIPS = sorted(
    [(dx, dy) for dx in range(4) for dy in range(4) if (dx, dy) != (0, 0)],
    key=lambda t: -(min(t[0], 4 - t[0]) + min(t[1], 4 - t[1])),
)


def local_copy(src, dst, sem):
    return pltpu.make_async_copy(src, dst, sem)


def settle(ref, sem):
    pltpu.make_async_copy(ref, ref, sem).wait()


def kernel(
    rhs, panel, solved, dinv, inner, out,
    lp, xs, p0, z0, ds, dq, wd, wl, mk, rv, own, part, rs, st, ga, rb, xout, xin, pend, pre,
    in_sem, p0_send, z0_recv, rs_send, rs_recv, g_send, g_recv, d_send, d_recv, m_send, m_recv, h_send, h_recv,
    w_send, w_recv, x_send, x_recv,
):
    r = lax.axis_index("row")
    c = lax.axis_index("col")
    k = r % 2
    p = r // 2
    y = p % 4
    x = p // 4
    sib = (2 * p + 1 - k, c)
    chips = [((x + dx) % 4) * 4 + (y + dy) % 4 for dx, dy in CHIPS]

    def send(src, dst, ssem, rsem, dev):
        pltpu.make_async_remote_copy(
            src_ref=src, dst_ref=dst, send_sem=ssem, recv_sem=rsem,
            device_id=dev, device_id_type=MESH,
        ).start()

    barrier = pltpu.get_barrier_semaphore()
    for off in range(1, 8):
        for row in (r, 2 * p + 1 - k):
            pl.semaphore_signal(barrier, inc=1, device_id=(row, (c + off) % 8), device_id_type=MESH)
    pl.semaphore_signal(barrier, inc=1, device_id=sib, device_id_type=MESH)
    for q in chips:
        for core in range(2):
            pl.semaphore_signal(barrier, inc=1, device_id=(2 * q + core, c), device_id_type=MESH)


    p_load = [
        local_copy(panel.at[0], lp.at[0], in_sem.at[0]),
        local_copy(panel.at[pl.ds(1, 3)], lp.at[pl.ds(1, 3)], in_sem.at[12]),
    ]
    x_load = []
    for i in range(4):
        for half, off in enumerate((4 + i, 3 - i)):
            dest = (c + off) % 8
            x_load.append(
                local_copy(
                    solved.at[:, pl.ds(pl.multiple_of(dest * 128, 128), 128)],
                    xs.at[i, :, pl.ds(128 * half, 128)],
                    in_sem.at[1 + 2 * i + half],
                )
            )
    r_load = local_copy(rhs, rv, in_sem.at[9])
    d_load = [local_copy(dinv.at[m], wd.at[m, k], in_sem.at[13 + m]) for m in range(4)]
    l_load = [
        local_copy(inner.at[pl.ds(0, 3)], wl.at[pl.ds(0, 3), k], in_sem.at[10]),
        local_copy(inner.at[pl.ds(3, 3)], wl.at[pl.ds(3, 3), k], in_sem.at[11]),
    ]
    slice_of = lambda core: jnp.where(core == 0, c, 15 - c)
    my_slice = slice_of(k)
    s_load = [
        local_copy(
            dinv.at[1 + j, :, pl.ds(pl.multiple_of(slice_of(core) * 128, 128), 128)],
            ds.at[j, core],
            in_sem.at[17 + 2 * j + core],
        )
        for j in range(2)
        for core in range(2)
    ]
    p_load[0].start()
    for cp in x_load[:4] + s_load[:2] + x_load[4:]:
        cp.start()
    for cp in [r_load, p_load[1]] + s_load[2:] + d_load[:1] + l_load + d_load[1:]:
        cp.start()

    @pl.loop(0, my_slice)
    def _(i):
        rows = pl.ds(pl.multiple_of(i * 128, 128), 128)
        for j in range(2):
            dq[j, rows, :] = jnp.zeros((128, 128), BF)

    def send_inverse(j, piece):
        rows = pl.ds(pl.multiple_of(r * 64, 64), 64)
        for d in range(2):
            core = (k + d) % 2
            s = slice_of(core)
            src = ds.at[j, core]
            dst = dq.at[j, rows]

            @pl.when(p >= s)
            def _():
                for q in chips[piece::3]:
                    send(src, dst, d_send.at[j], d_recv.at[j], (2 * q + core, c))
                if piece > 0:
                    return
                if d == 0:
                    local_copy(src, dst, d_recv.at[j]).start()
                else:
                    send(src, dst, d_send.at[j], d_recv.at[j], sib)

    def sent_inverse(j):
        near, far = p >= slice_of(k), p >= slice_of(1 - k)
        for rows, cond in (
            (1984, near & far),
            (960, near & jnp.logical_not(far)),
            (1024, far & jnp.logical_not(near)),
        ):

            @pl.when(cond)
            def _():
                settle(dq.at[j, pl.ds(0, rows)], d_send.at[j])

    def got_inverse(j):
        for s in range(16):

            @pl.when(my_slice == s)
            def _():
                settle(dq.at[j, pl.ds(128 * s, 2048 - 128 * s)], d_recv.at[j])

    def send_weights():
        send(dinv.at[0], wd.at[0, k], w_send.at[0], w_recv.at[0], sib)
        send(inner.at[pl.ds(0, 3)], wl.at[pl.ds(0, 3), k], w_send.at[1], w_recv.at[1], sib)
        send(inner.at[pl.ds(3, 3)], wl.at[pl.ds(3, 3), k], w_send.at[2], w_recv.at[2], sib)
        send(dinv.at[pl.ds(1, 3)], wd.at[pl.ds(1, 3), k], w_send.at[3], w_recv.at[3], sib)

    def pass_on(i, plane, off, e):
        slot = jnp.where(k == 0, plane % 8, 15 - plane % 8)
        send(
            mk.at[i, slot], mk.at[i, slot], m_send.at[i, e], m_recv.at[i, e], (r, (c + off) % 8)
        )

    def make_product(i, n, j):
        mk[i, my_slice] = dot(wl[n].reshape(128, 2048), dq[j]).astype(BF)
        for off in (2, 6, 1, 7):
            pass_on(i, c, off, 0)

    def relay_product(i):
        settle(mk.at[i, pl.ds(0, 4)], m_recv.at[i, 0])
        far = 2 + 4 * k
        pass_on(i, c + 8 - far, far, 1)
        pass_on(i, c + 6, 1, 1)
        pass_on(i, c + 2, 7, 1)

    def share_product(i):
        settle(mk.at[i, pl.ds(0, 3)], m_recv.at[i, 1])
        part_cols = mk.at[i, pl.ds(8 * k, 8)]
        send(part_cols, part_cols, h_send.at[i], h_recv.at[i], sib)

    def got_product(i):
        settle(mk.at[i, pl.ds(0, 8)], h_recv.at[i])

    def rs_send_one(off, m):
        send(part.at[off, m], rs.at[m, off - 1], rs_send, rs_recv.at[m], (r, (c + off) % 8))

    def rs_send_all(m, offs=(4, 5, 3, 6, 2, 7, 1)):
        for off in offs:
            rs_send_one(off, m)

    lane = lax.broadcasted_iota(jnp.int32, (64, 128), 1)
    left = lane < 64
    stay = left == (k == 0)

    def product(i, lo, hi):
        rows = 64 * (hi - lo)
        acc = dot(lp[lo:hi].reshape(rows, 4096), xs[i]).reshape(hi - lo, 64, 256)
        return acc[:, :, :128], acc[:, :, 128:]

    def product_later(i):
        first, second = product(i, 1, 4)
        part[4 + i, 1:] = first.astype(BF)
        if i < 3:
            part[3 - i, 1:] = second.astype(BF)
        else:
            own[1:] = second

    def fold(value):
        top, low = value[0, :32], value[0, 32:]
        return (
            jnp.where(left[:32], top, pltpu.roll(low, 64, 1)),
            jnp.where(left[:32], pltpu.roll(top, 64, 1), low),
        )

    def product_first(i):
        for off, value in zip((4 + i, 3 - i), product(i, 0, 1)):
            for core, folded in enumerate(fold(value)):
                p0[2 * off + core] = folded.astype(BF)
                if off == 0:
                    xout[7 + core, :32] = folded

    def rs_chunk(i):
        for off in (4 + i, 3 - i):
            dst = z0.at[8 * k + off]
            if off:
                send(p0.at[2 * off + k], dst, p0_send, z0_recv, (r, (c + off) % 8))
            send(p0.at[2 * off + 1 - k], dst, p0_send, z0_recv, (2 * p + 1 - k, (c + off) % 8))

    def reduce_first():
        settle(z0.at[pl.ds(0, 15)], z0_recv)
        mine = xout[7 + k, :32]
        for off in range(1, 8):
            mine = mine + z0[8 * k + off].astype(F32)
        theirs = z0[8 * (1 - k)].astype(F32)
        for off in range(1, 8):
            theirs = theirs + z0[8 * (1 - k) + off].astype(F32)
        first = jnp.where(k == 0, mine, theirs)
        second = jnp.where(k == 0, theirs, mine)
        return jnp.concatenate(
            [
                jnp.where(left[:32], first, pltpu.roll(second, 64, 1)),
                jnp.where(left[:32], pltpu.roll(first, 64, 1), second),
            ],
            axis=0,
        )

    def turn_start(e, value):
        xout[e] = pltpu.roll(value, 64, 1)
        send(xout.at[e], xin.at[e], x_send.at[e], x_recv.at[e], sib)

    def turn_end(e, value):
        settle(xin.at[e], x_recv.at[e])
        return jnp.where(stay, value, xin[e])

    def turn(e, value):
        turn_start(e, value)
        return turn_end(e, value)

    p_load[0].wait()
    for i in range(4):
        x_load[2 * i].wait()
        x_load[2 * i + 1].wait()
        product_first(i)
        if i == 1:
            pl.semaphore_wait(barrier, 45)
            rs_chunk(0)
        if i >= 1:
            rs_chunk(i)
        if i == 1:
            s_load[0].wait()
            s_load[1].wait()
            send_weights()
        if i >= 1:
            send_inverse(0, i - 1)
    r_load.wait()
    turn_start(0, rv[0])
    p_load[1].wait()
    for i in range(3):
        product_later(i)
    for m in (1, 2):
        rs_send_all(m, (4, 5, 3, 6, 2, 1))

    def reduce(m):
        settle(rs.at[m], rs_recv.at[m])
        total = own[m]
        for s in range(7):
            total = total + rs[m, s].astype(F32)
        return rv[m] - total

    slot = pl.ds(pl.multiple_of(p * 64, 64), 64)

    def spread(n, value):
        st[n] = value.astype(BF)
        for q in chips:
            send(st.at[n], ga.at[n, slot], g_send.at[n], g_recv.at[n], (2 * q + k, c))
        local_copy(st.at[n], ga.at[n, slot], g_recv.at[n]).start()

    def arrived(n):
        settle(ga.at[n], g_recv.at[n])
        here = ga[n]
        there = pltpu.roll(here, 64, 1).reshape(16, 64, 128)
        here = here.reshape(16, 64, 128)
        rb[:, 0, :, :128] = here
        rb[:, 1, :, :128] = there
        rb[:, 0, :, 128:] = there
        rb[:, 1, :, 128:] = here

    def joined(i):
        return jnp.concatenate([mk[i, q] for q in range(16)], axis=1)

    def apply(w):
        prod = dot(w.reshape(128, 2048), rb[...].reshape(2048, 256))
        return jnp.where(left, prod[:64, :128], prod[64:, 128:])

    spread(0, turn_end(0, rv[0]) - reduce_first())
    product_later(3)
    for m in (1, 2):
        rs_send_all(m, (7,))
    for cp in s_load[2:] + d_load + l_load:
        cp.wait()
    settle(wd.at[0, 0], w_recv.at[0])
    settle(wl.at[pl.ds(0, 3), 0], w_recv.at[1])
    settle(wl.at[pl.ds(3, 3), 0], w_recv.at[2])
    settle(wd.at[pl.ds(1, 3), 0], w_recv.at[3])
    got_inverse(0)
    make_product(0, LATER[0], 0)
    for piece in range(3):
        send_inverse(1, piece)
    rs_send_all(3)

    arrived(0)
    sol = apply(wd[0])
    spread(1, sol)
    turn_start(4, sol)
    make_product(1, LATER[1], 0)
    pend[1] = reduce(1)
    turn_start(1, pend[1])
    out[0] = turn_end(4, sol)
    relay_product(0)
    got_inverse(1)
    make_product(2, LATER[2], 1)

    arrived(1)
    spread(2, turn_end(1, pend[1]) - apply(wl[FIRST[0]]))
    relay_product(1)
    pend[2] = reduce(2)
    turn_start(2, pend[2])
    share_product(0)
    pre[...] = apply(wl[FIRST[2]])
    pend[2] = turn_end(2, pend[2]) - apply(wl[FIRST[1]])
    got_product(0)
    relay_product(2)

    for m in (1, 2):
        arrived(m + 1)
        spread(m + 2, pend[m + 1] - apply(joined(2 * m - 2)))
        sol = apply(wd[m])
        turn_start(4 + m, sol)
        if m == 1:
            share_product(1)
            pend[3] = reduce(3)
            turn_start(3, pend[3])
            got_product(1)
            pre[...] = pre[...] + apply(joined(1))
            share_product(2)
            pend[3] = turn_end(3, pend[3]) - pre[...]
        out[m] = turn_end(4 + m, sol)
        if m == 1:
            got_product(2)

    arrived(4)
    sides = rb.at[:, :, :, pl.ds(pl.multiple_of(128 * (1 - k), 128), 128)]
    turn_start(7, dot(wd[3, 1 - k], sides[...].reshape(2048, 128)))
    sides = rb.at[:, :, :, pl.ds(pl.multiple_of(128 * k, 128), 128)]
    out[3] = turn_end(7, dot(wd[3, k], sides[...].reshape(2048, 128)))

    settle(part.at[pl.ds(1, 7), pl.ds(1, 3)], rs_send)
    settle(p0.at[pl.ds(0, 15)], p0_send)
    for n in range(5):
        settle(ga.at[n, pl.ds(0, 960)], g_send.at[n])
    for j in range(2):
        sent_inverse(j)
    for i in range(3):
        settle(mk.at[i, pl.ds(0, 4)], m_send.at[i, 0])
        settle(mk.at[i, pl.ds(0, 3)], m_send.at[i, 1])
        settle(mk.at[i, pl.ds(0, 8)], h_send.at[i])
    settle(wd.at[0, 0], w_send.at[0])
    settle(wl.at[pl.ds(0, 3), 0], w_send.at[1])
    settle(wl.at[pl.ds(3, 3), 0], w_send.at[2])
    settle(wd.at[pl.ds(1, 3), 0], w_send.at[3])
    for e in range(8):
        settle(xin.at[e], x_send.at[e])


def local(rhs, l_panel, x_solved, diag_inv, l_inner):
    any_spec = pl.BlockSpec(memory_space=pl.ANY)
    dma = pltpu.SemaphoreType.DMA
    return pl.pallas_call(
        kernel,
        out_shape=pltpu.VMEM((4, 64, 128), F32),
        in_specs=[any_spec] * 5,
        out_specs=pl.BlockSpec(memory_space=pltpu.VMEM),
        scratch_shapes=[
            pltpu.VMEM((4, 64, 4096), BF),
            pltpu.VMEM((4, 4096, 256), BF),
            pltpu.VMEM((16, 32, 128), BF),
            pltpu.VMEM((16, 32, 128), BF),
            pltpu.VMEM((2, 2, 64, 128), BF),
            pltpu.VMEM((2, 2048, 128), BF),
            pltpu.VMEM((4, 2, 64, 2048), BF),
            pltpu.VMEM((6, 2, 64, 2048), BF),
            pltpu.VMEM((3, 16, 128, 128), BF),
            pltpu.VMEM((4, 64, 128), F32),
            pltpu.VMEM((4, 64, 128), F32),
            pltpu.VMEM((8, 4, 64, 128), BF),
            pltpu.VMEM((4, 7, 64, 128), BF),
            pltpu.VMEM((5, 64, 128), BF),
            pltpu.VMEM((5, 1024, 128), BF),
            pltpu.VMEM((16, 2, 64, 256), BF),
            pltpu.VMEM((9, 64, 128), F32),
            pltpu.VMEM((8, 64, 128), F32),
            pltpu.VMEM((4, 64, 128), F32),
            pltpu.VMEM((64, 128), F32),
            dma((21,)),
            dma,
            dma,
            dma,
            dma((4,)),
            dma((5,)),
            dma((5,)),
            dma((2,)),
            dma((2,)),
            dma((3, 2)),
            dma((3, 2)),
            dma((3,)),
            dma((3,)),
            dma((4,)),
            dma((4,)),
            dma((8,)),
            dma((8,)),
        ],
        compiler_params=pltpu.CompilerParams(
            collective_id=0, has_side_effects=True, vmem_limit_bytes=60 * 1024 * 1024
        ),
    )(rhs, l_panel, x_solved, diag_inv, l_inner)


def solution(mesh):
    in_specs = (
        P(None, "row", "col"),
        P(None, "row", "col"),
        P("col", None),
        P(None, "row", None),
        P(None, "row", None),
    )
    return jax.shard_map(
        local, mesh=mesh, in_specs=in_specs, out_specs=P(None, "row", "col"), check_vma=False
    )
```

```python
import jax
import jax.numpy as jnp
from jax import lax
from jax.experimental import pallas as pl
from jax.experimental.pallas import tpu as pltpu
from jax.sharding import PartitionSpec as P

MESH = pl.DeviceIdType.MESH
BF = jnp.bfloat16
F32 = jnp.float32


def dot(a, b):
    return jnp.dot(a, b, preferred_element_type=F32)


FIRST = (0, 1, 3)
LATER = (2, 4, 5)

CHIPS = sorted(
    [(dx, dy) for dx in range(4) for dy in range(4) if (dx, dy) != (0, 0)],
    key=lambda t: -(min(t[0], 4 - t[0]) + min(t[1], 4 - t[1])),
)


def local_copy(src, dst, sem):
    return pltpu.make_async_copy(src, dst, sem)


def settle(ref, sem):
    pltpu.make_async_copy(ref, ref, sem).wait()


def kernel(
    rhs, panel, solved, dinv, inner, out,
    lp, xs, p0, z0, ds, dq, wd, wl, mk, rv, own, part, rs, st, ga, rb, xout, xin, pend, pre,
    in_sem, p0_send, z0_recv, rs_send, rs_recv, g_send, g_recv, d_send, d_recv, m_send, m_recv, h_send, h_recv,
    w_send, w_recv, x_send, x_recv,
):
    r = lax.axis_index("row")
    c = lax.axis_index("col")
    k = r % 2
    p = r // 2
    y = p % 4
    x = p // 4
    sib = (2 * p + 1 - k, c)
    chips = [((x + dx) % 4) * 4 + (y + dy) % 4 for dx, dy in CHIPS]

    def send(src, dst, ssem, rsem, dev):
        pltpu.make_async_remote_copy(
            src_ref=src, dst_ref=dst, send_sem=ssem, recv_sem=rsem,
            device_id=dev, device_id_type=MESH,
        ).start()

    barrier = pltpu.get_barrier_semaphore()
    for off in range(1, 8):
        for row in (r, 2 * p + 1 - k):
            pl.semaphore_signal(barrier, inc=1, device_id=(row, (c + off) % 8), device_id_type=MESH)
    pl.semaphore_signal(barrier, inc=1, device_id=sib, device_id_type=MESH)
    for q in chips:
        for core in range(2):
            pl.semaphore_signal(barrier, inc=1, device_id=(2 * q + core, c), device_id_type=MESH)


    p_load = [
        local_copy(panel.at[0], lp.at[0], in_sem.at[0]),
        local_copy(panel.at[pl.ds(1, 3)], lp.at[pl.ds(1, 3)], in_sem.at[12]),
    ]
    x_load = []
    for i in range(4):
        for half, off in enumerate((4 + i, 3 - i)):
            dest = (c + off) % 8
            x_load.append(
                local_copy(
                    solved.at[:, pl.ds(pl.multiple_of(dest * 128, 128), 128)],
                    xs.at[i, :, pl.ds(128 * half, 128)],
                    in_sem.at[1 + 2 * i + half],
                )
            )
    r_load = local_copy(rhs, rv, in_sem.at[9])
    d_load = [local_copy(dinv.at[m], wd.at[m, k], in_sem.at[13 + m]) for m in range(4)]
    l_load = [
        local_copy(inner.at[pl.ds(0, 3)], wl.at[pl.ds(0, 3), k], in_sem.at[10]),
        local_copy(inner.at[pl.ds(3, 3)], wl.at[pl.ds(3, 3), k], in_sem.at[11]),
    ]
    slice_of = lambda core: jnp.where(core == 0, c, 15 - c)
    my_slice = slice_of(k)
    s_load = [
        local_copy(
            dinv.at[1 + j, :, pl.ds(pl.multiple_of(slice_of(core) * 128, 128), 128)],
            ds.at[j, core],
            in_sem.at[17 + 2 * j + core],
        )
        for j in range(2)
        for core in range(2)
    ]
    p_load[0].start()
    for cp in x_load[:4] + s_load[:2] + x_load[4:]:
        cp.start()
    for cp in [r_load, p_load[1]] + s_load[2:] + d_load[:1] + l_load + d_load[1:]:
        cp.start()

    @pl.loop(0, my_slice)
    def _(i):
        rows = pl.ds(pl.multiple_of(i * 128, 128), 128)
        for j in range(2):
            dq[j, rows, :] = jnp.zeros((128, 128), BF)

    def send_inverse(j, piece):
        rows = pl.ds(pl.multiple_of(r * 64, 64), 64)
        for d in range(2):
            core = (k + d) % 2
            s = slice_of(core)
            src = ds.at[j, core]
            dst = dq.at[j, rows]

            @pl.when(p >= s)
            def _():
                for q in chips[piece::3]:
                    send(src, dst, d_send.at[j], d_recv.at[j], (2 * q + core, c))
                if piece > 0:
                    return
                if d == 0:
                    local_copy(src, dst, d_recv.at[j]).start()
                else:
                    send(src, dst, d_send.at[j], d_recv.at[j], sib)

    def sent_inverse(j):
        near, far = p >= slice_of(k), p >= slice_of(1 - k)
        for rows, cond in (
            (1984, near & far),
            (960, near & jnp.logical_not(far)),
            (1024, far & jnp.logical_not(near)),
        ):

            @pl.when(cond)
            def _():
                settle(dq.at[j, pl.ds(0, rows)], d_send.at[j])

    def got_inverse(j):
        for s in range(16):

            @pl.when(my_slice == s)
            def _():
                settle(dq.at[j, pl.ds(128 * s, 2048 - 128 * s)], d_recv.at[j])

    def send_weights():
        send(dinv.at[0], wd.at[0, k], w_send.at[0], w_recv.at[0], sib)
        send(inner.at[pl.ds(0, 3)], wl.at[pl.ds(0, 3), k], w_send.at[1], w_recv.at[1], sib)
        send(inner.at[pl.ds(3, 3)], wl.at[pl.ds(3, 3), k], w_send.at[2], w_recv.at[2], sib)
        send(dinv.at[pl.ds(1, 3)], wd.at[pl.ds(1, 3), k], w_send.at[3], w_recv.at[3], sib)

    def pass_on(i, plane, off, e):
        slot = jnp.where(k == 0, plane % 8, 15 - plane % 8)
        send(
            mk.at[i, slot], mk.at[i, slot], m_send.at[i, e], m_recv.at[i, e], (r, (c + off) % 8)
        )

    def make_product(i, n, j):
        mk[i, my_slice] = dot(wl[n].reshape(128, 2048), dq[j]).astype(BF)
        for off in (2, 6, 1, 7):
            pass_on(i, c, off, 0)

    def relay_product(i):
        settle(mk.at[i, pl.ds(0, 4)], m_recv.at[i, 0])
        far = 2 + 4 * k
        pass_on(i, c + 8 - far, far, 1)
        pass_on(i, c + 6, 1, 1)
        pass_on(i, c + 2, 7, 1)

    def share_product(i):
        settle(mk.at[i, pl.ds(0, 3)], m_recv.at[i, 1])
        part_cols = mk.at[i, pl.ds(8 * k, 8)]
        send(part_cols, part_cols, h_send.at[i], h_recv.at[i], sib)

    def got_product(i):
        settle(mk.at[i, pl.ds(0, 8)], h_recv.at[i])

    def rs_send_one(off, m):
        send(part.at[off, m], rs.at[m, off - 1], rs_send, rs_recv.at[m], (r, (c + off) % 8))

    def rs_send_all(m, offs=(4, 5, 3, 6, 2, 7, 1)):
        for off in offs:
            rs_send_one(off, m)

    lane = lax.broadcasted_iota(jnp.int32, (64, 128), 1)
    left = lane < 64
    stay = left == (k == 0)

    def product(i, lo, hi):
        rows = 64 * (hi - lo)
        acc = dot(lp[lo:hi].reshape(rows, 4096), xs[i]).reshape(hi - lo, 64, 256)
        return acc[:, :, :128], acc[:, :, 128:]

    def product_later(i):
        first, second = product(i, 1, 4)
        part[4 + i, 1:] = first.astype(BF)
        if i < 3:
            part[3 - i, 1:] = second.astype(BF)
        else:
            own[1:] = second

    def fold(value):
        top, low = value[0, :32], value[0, 32:]
        return (
            jnp.where(left[:32], top, pltpu.roll(low, 64, 1)),
            jnp.where(left[:32], pltpu.roll(top, 64, 1), low),
        )

    def product_first(i):
        for off, value in zip((4 + i, 3 - i), product(i, 0, 1)):
            for core, folded in enumerate(fold(value)):
                p0[2 * off + core] = folded.astype(BF)
                if off == 0:
                    xout[7 + core, :32] = folded

    def rs_chunk(i):
        for off in (4 + i, 3 - i):
            dst = z0.at[8 * k + off]
            if off:
                send(p0.at[2 * off + k], dst, p0_send, z0_recv, (r, (c + off) % 8))
            send(p0.at[2 * off + 1 - k], dst, p0_send, z0_recv, (2 * p + 1 - k, (c + off) % 8))

    def reduce_first():
        settle(z0.at[pl.ds(0, 15)], z0_recv)
        mine = xout[7 + k, :32]
        for off in range(1, 8):
            mine = mine + z0[8 * k + off].astype(F32)
        theirs = z0[8 * (1 - k)].astype(F32)
        for off in range(1, 8):
            theirs = theirs + z0[8 * (1 - k) + off].astype(F32)
        first = jnp.where(k == 0, mine, theirs)
        second = jnp.where(k == 0, theirs, mine)
        return jnp.concatenate(
            [
                jnp.where(left[:32], first, pltpu.roll(second, 64, 1)),
                jnp.where(left[:32], pltpu.roll(first, 64, 1), second),
            ],
            axis=0,
        )

    def turn_start(e, value):
        xout[e] = pltpu.roll(value, 64, 1)
        send(xout.at[e], xin.at[e], x_send.at[e], x_recv.at[e], sib)

    def turn_end(e, value):
        settle(xin.at[e], x_recv.at[e])
        return jnp.where(stay, value, xin[e])

    def turn(e, value):
        turn_start(e, value)
        return turn_end(e, value)

    p_load[0].wait()
    for i in range(4):
        x_load[2 * i].wait()
        x_load[2 * i + 1].wait()
        product_first(i)
        if i == 1:
            pl.semaphore_wait(barrier, 45)
            rs_chunk(0)
        if i >= 1:
            rs_chunk(i)
        if i == 1:
            s_load[0].wait()
            s_load[1].wait()
            send_weights()
        if i >= 1:
            send_inverse(0, i - 1)
    r_load.wait()
    turn_start(0, rv[0])
    p_load[1].wait()
    for i in range(3):
        product_later(i)
    for m in (1, 2):
        rs_send_all(m, (4, 5, 3, 6, 2, 1))

    def reduce(m):
        settle(rs.at[m], rs_recv.at[m])
        total = own[m]
        for s in range(7):
            total = total + rs[m, s].astype(F32)
        return rv[m] - total

    slot = pl.ds(pl.multiple_of(p * 64, 64), 64)

    def spread(n, value):
        st[n] = value.astype(BF)
        for q in chips:
            send(st.at[n], ga.at[n, slot], g_send.at[n], g_recv.at[n], (2 * q + k, c))
        local_copy(st.at[n], ga.at[n, slot], g_recv.at[n]).start()

    def arrived(n):
        settle(ga.at[n], g_recv.at[n])
        here = ga[n]
        there = pltpu.roll(here, 64, 1).reshape(16, 64, 128)
        here = here.reshape(16, 64, 128)
        rb[:, 0, :, :128] = here
        rb[:, 1, :, :128] = there
        rb[:, 0, :, 128:] = there
        rb[:, 1, :, 128:] = here

    def joined(i):
        return jnp.concatenate([mk[i, q] for q in range(16)], axis=1)

    def apply(w):
        prod = dot(w.reshape(128, 2048), rb[...].reshape(2048, 256))
        return jnp.where(left, prod[:64, :128], prod[64:, 128:])

    spread(0, turn_end(0, rv[0]) - reduce_first())
    product_later(3)
    for m in (1, 2):
        rs_send_all(m, (7,))
    for cp in s_load[2:] + d_load + l_load:
        cp.wait()
    settle(wd.at[0, 0], w_recv.at[0])
    settle(wl.at[pl.ds(0, 3), 0], w_recv.at[1])
    settle(wl.at[pl.ds(3, 3), 0], w_recv.at[2])
    settle(wd.at[pl.ds(1, 3), 0], w_recv.at[3])
    got_inverse(0)
    make_product(0, LATER[0], 0)
    for piece in range(3):
        send_inverse(1, piece)
    make_product(1, LATER[1], 0)

    arrived(0)
    sol = apply(wd[0])
    spread(1, sol)
    turn_start(4, sol)
    rs_send_all(3)
    pend[1] = reduce(1)
    turn_start(1, pend[1])
    out[0] = turn_end(4, sol)
    relay_product(0)
    got_inverse(1)
    make_product(2, LATER[2], 1)

    arrived(1)
    spread(2, turn_end(1, pend[1]) - apply(wl[FIRST[0]]))
    relay_product(1)
    pend[2] = reduce(2)
    turn_start(2, pend[2])
    share_product(0)
    pre[...] = apply(wl[FIRST[2]])
    pend[2] = turn_end(2, pend[2]) - apply(wl[FIRST[1]])
    got_product(0)
    relay_product(2)

    for m in (1, 2):
        arrived(m + 1)
        spread(m + 2, pend[m + 1] - apply(joined(2 * m - 2)))
        sol = apply(wd[m])
        turn_start(4 + m, sol)
        if m == 1:
            share_product(1)
            pend[3] = reduce(3)
            turn_start(3, pend[3])
            got_product(1)
            pre[...] = pre[...] + apply(joined(1))
            share_product(2)
            pend[3] = turn_end(3, pend[3]) - pre[...]
        out[m] = turn_end(4 + m, sol)
        if m == 1:
            got_product(2)

    arrived(4)
    sides = rb.at[:, :, :, pl.ds(pl.multiple_of(128 * (1 - k), 128), 128)]
    turn_start(7, dot(wd[3, 1 - k], sides[...].reshape(2048, 128)))
    sides = rb.at[:, :, :, pl.ds(pl.multiple_of(128 * k, 128), 128)]
    out[3] = turn_end(7, dot(wd[3, k], sides[...].reshape(2048, 128)))

    settle(part.at[pl.ds(1, 7), pl.ds(1, 3)], rs_send)
    settle(p0.at[pl.ds(0, 15)], p0_send)
    for n in range(5):
        settle(ga.at[n, pl.ds(0, 960)], g_send.at[n])
    for j in range(2):
        sent_inverse(j)
    for i in range(3):
        settle(mk.at[i, pl.ds(0, 4)], m_send.at[i, 0])
        settle(mk.at[i, pl.ds(0, 3)], m_send.at[i, 1])
        settle(mk.at[i, pl.ds(0, 8)], h_send.at[i])
    settle(wd.at[0, 0], w_send.at[0])
    settle(wl.at[pl.ds(0, 3), 0], w_send.at[1])
    settle(wl.at[pl.ds(3, 3), 0], w_send.at[2])
    settle(wd.at[pl.ds(1, 3), 0], w_send.at[3])
    for e in range(8):
        settle(xin.at[e], x_send.at[e])


def local(rhs, l_panel, x_solved, diag_inv, l_inner):
    any_spec = pl.BlockSpec(memory_space=pl.ANY)
    dma = pltpu.SemaphoreType.DMA
    return pl.pallas_call(
        kernel,
        out_shape=pltpu.VMEM((4, 64, 128), F32),
        in_specs=[any_spec] * 5,
        out_specs=pl.BlockSpec(memory_space=pltpu.VMEM),
        scratch_shapes=[
            pltpu.VMEM((4, 64, 4096), BF),
            pltpu.VMEM((4, 4096, 256), BF),
            pltpu.VMEM((16, 32, 128), BF),
            pltpu.VMEM((16, 32, 128), BF),
            pltpu.VMEM((2, 2, 64, 128), BF),
            pltpu.VMEM((2, 2048, 128), BF),
            pltpu.VMEM((4, 2, 64, 2048), BF),
            pltpu.VMEM((6, 2, 64, 2048), BF),
            pltpu.VMEM((3, 16, 128, 128), BF),
            pltpu.VMEM((4, 64, 128), F32),
            pltpu.VMEM((4, 64, 128), F32),
            pltpu.VMEM((8, 4, 64, 128), BF),
            pltpu.VMEM((4, 7, 64, 128), BF),
            pltpu.VMEM((5, 64, 128), BF),
            pltpu.VMEM((5, 1024, 128), BF),
            pltpu.VMEM((16, 2, 64, 256), BF),
            pltpu.VMEM((9, 64, 128), F32),
            pltpu.VMEM((8, 64, 128), F32),
            pltpu.VMEM((4, 64, 128), F32),
            pltpu.VMEM((64, 128), F32),
            dma((21,)),
            dma,
            dma,
            dma,
            dma((4,)),
            dma((5,)),
            dma((5,)),
            dma((2,)),
            dma((2,)),
            dma((3, 2)),
            dma((3, 2)),
            dma((3,)),
            dma((3,)),
            dma((4,)),
            dma((4,)),
            dma((8,)),
            dma((8,)),
        ],
        compiler_params=pltpu.CompilerParams(
            collective_id=0, has_side_effects=True, vmem_limit_bytes=60 * 1024 * 1024
        ),
    )(rhs, l_panel, x_solved, diag_inv, l_inner)


def solution(mesh):
    in_specs = (
        P(None, "row", "col"),
        P(None, "row", "col"),
        P("col", None),
        P(None, "row", None),
        P(None, "row", None),
    )
    return jax.shard_map(
        local, mesh=mesh, in_specs=in_specs, out_specs=P(None, "row", "col"), check_vma=False
    )
```
